512 devices in a mesh: seq: 64 (over y, x, z_hi), tp: 8 (over z_lo, core).
Axes of the slice: x: 4, y: 8, z: 8 (z_hi: 2, z_lo: 4; z = z_hi * 4 + z_lo), core: 2. Of those that a mesh axis runs over, the one named last changes fastest.
Arguments:
- hidden_in: bfloat16 [16384, 2048], P('seq', 'tp'), may hold values from -6 to 6
- w_query: bfloat16 [2048, 2048], P(None, 'tp'), may hold values from -0.375 to 0.375
- w_keyval: bfloat16 [2048, 2, 2048], P(None, None, 'tp'), may hold values from -0.125 to 0.125
- w_out: bfloat16 [2048, 2048], P('tp'), may hold values from -0.125 to 0.125
- prompt_cache: bfloat16 [8192, 2, 2048], P('seq', None, 'tp'), may hold values from -160 to 160
- tail_cache: bfloat16 [128, 128, 2, 2048], P('seq', None, None, 'tp'), may hold values from -6 to 6
- tail_table: int32 [8, 16], replicated, may hold values from 0 to 127, as said below
- tail_len: int32 [8], replicated, may hold values from 1 to 2048
- shared_len: int32 [1], replicated, may hold values from 4096 to 8192
Outputs:
- hidden_out: bfloat16 [16384, 2048], P('seq', 'tp')
- new_cache: bfloat16 [16384, 2, 2048], P('seq', None, 'tp')
The draws below stay inside these ranges and needn't reach their ends.
Inputs may be any that keep to these rules, and one draw needn't show every extreme that they name: Row r lists each of the slots r * 16 to (r + 1) * 16 - 1 once; block j of request r's tail is held in slot tail_table[r, j].
All inputs are finite; a program needn't handle non-finite values.
Results may differ from the reference program's by a relative error of at most 0.013.
Values may be sent and summed in bfloat16 or wider, within the bound.
A program may use at most 128 MiB of HBM per device.

```python
import jax
import jax.numpy as jnp
from jax import lax

D = 2048
HEADS = 16
HD = 128
REQ = 8
BLK = 128
FRESH = 2048
TOKENS = 16384
PROMPT = 8192
SLOTS = 128
TBLK = 16
TAIL = 2048


def draw_prompt_cache(key, part):
    base = jnp.clip(jax.random.normal(key, (PROMPT, 2, HEADS * HD), jnp.float32), -6.0, 6.0)
    return base.astype(jnp.bfloat16)


def order_slots(subkey):
    return jax.random.permutation(subkey, TBLK)


def draw_tail_table(key, part):
    orders = jax.vmap(order_slots)(jax.random.split(key, REQ))
    return (jnp.arange(REQ, dtype=jnp.int32)[:, None] * TBLK + orders).astype(jnp.int32)


def set_ends(values, own_key, smallest, high):
    shape = values.shape
    index_at = [jax.random.randint(jax.random.fold_in(own_key, axis), (), 0, shape[axis]) for axis in range(len(shape))]
    values = values.at[tuple(index_at)].set(smallest)
    longest = shape.index(max(shape))
    index_at[longest] = (index_at[longest] + 1) % shape[longest]
    return values.at[tuple(index_at)].set(high)


def levels(key, shape, shards, smallest, high):
    def one(dim, parts):
        draws = jax.random.uniform(jax.random.fold_in(jax.random.fold_in(key, 6), dim), (parts,), jnp.float32, smallest / len(shards), high / len(shards))
        return jnp.repeat(jnp.exp(draws), shape[dim] // parts).reshape((-1,) + (1,) * (len(shape) - dim - 1))

    gain = one(*shards[0])
    for cut in shards[1:]:
        gain = gain * one(*cut)
    return gain


def scatter_about(stream_key, shape, scale, most, cuts=(), kind=jnp.bfloat16):
    entries = scale * jax.random.normal(stream_key, shape, jnp.float32)
    if cuts:
        entries = entries * levels(stream_key, shape, cuts, -0.22, 0.18)
    return jnp.clip(entries, -most, most).astype(kind)


def setup_inputs(seed: int = 0) -> dict:
    seeds = jax.random.split(jax.random.key(seed), 10)
    return {
        "hidden_in": scatter_about(seeds[0], (TOKENS, D), 1.0, 6.0, ((0, 64), (1, 8))),
        "w_query": scatter_about(seeds[1], (D, HEADS * HD), (D // 9) ** -0.5, 0.375, ((1, 8),)),
        "w_keyval": scatter_about(seeds[2], (D, 2, HEADS * HD), D ** -0.5, 0.125, ((2, 8),)),
        "w_out": scatter_about(seeds[3], (HEADS * HD, D), (HEADS * HD) ** -0.5, 0.125, ((0, 8),)),
        "prompt_cache": draw_prompt_cache(jax.random.fold_in(seeds[9], 71), 0),
        "tail_cache": scatter_about(seeds[5], (SLOTS, BLK, 2, HEADS * HD), 1.0, 6.0, ((0, 64), (3, 8))),
        "tail_table": draw_tail_table(jax.random.fold_in(seeds[9], 71), 0),
        "tail_len": set_ends(jax.random.randint(seeds[7], (REQ,), 1, TAIL + 1), jax.random.fold_in(seeds[7], 1), 1, TAIL).astype(jnp.int32),
        "shared_len": jax.random.randint(seeds[8], (1,), PROMPT // 2, PROMPT + 1).astype(jnp.int32),
    }


def layer_norm(inputs):
    values = inputs.astype(jnp.float32)
    mean = lax.optimization_barrier(jnp.mean(values, axis=-1, keepdims=True))
    centred = values - mean
    spread = lax.optimization_barrier(jnp.mean(centred * centred, axis=-1, keepdims=True))
    return (centred * lax.rsqrt(spread + 1e-05)).astype(jnp.bfloat16)

def rotate(vectors, positions):
    half = vectors.shape[-1] // 2
    freqs = 10000.0 ** (-jnp.arange(half, dtype=jnp.float32) / half)
    angles = positions.astype(jnp.float32)[:, None, None] * freqs
    cosine = jnp.cos(angles)
    sine = jnp.sin(angles)
    first = vectors[..., :half]
    second = vectors[..., half:]
    return jnp.concatenate([first * cosine - second * sine, second * cosine + first * sine], axis=-1)

def attend_head(query, keys, values, allowed):
    scores = jnp.dot(query, keys.T, preferred_element_type=jnp.float32) * HD ** (-0.5)
    scores = jnp.where(allowed, scores, -jnp.inf)
    top = lax.optimization_barrier(jnp.max(scores, axis=1, keepdims=True))
    weights = jnp.exp(scores - top)
    total = lax.optimization_barrier(jnp.sum(weights, axis=1, keepdims=True))
    mixed = jnp.dot(weights.astype(jnp.bfloat16), values, preferred_element_type=jnp.float32)
    return (mixed / total).astype(jnp.bfloat16)

def reference(hidden_in, w_query, w_keyval, w_out, prompt_cache, tail_cache, tail_table, tail_len, shared_len):
    normed = layer_norm(hidden_in)
    query = jnp.dot(normed, w_query, preferred_element_type=jnp.float32).reshape(TOKENS, HEADS, HD)
    projected = jnp.dot(normed, w_keyval.reshape(D, 2 * HEADS * HD), preferred_element_type=jnp.float32)
    projected = projected.reshape(TOKENS, 2, HEADS, HD)
    token = jnp.arange(TOKENS, dtype=jnp.int32)
    request = token // FRESH
    prompt_length = shared_len[0]
    positions = prompt_length + tail_len[request] + token % FRESH
    query = rotate(query, positions).astype(jnp.bfloat16)
    new_keys = rotate(projected[:, 0], positions).astype(jnp.bfloat16)
    new_values = projected[:, 1].astype(jnp.bfloat16)
    new_cache = jnp.stack([new_keys.reshape(TOKENS, HEADS * HD), new_values.reshape(TOKENS, HEADS * HD)], axis=1)
    tails = tail_cache[tail_table].reshape(REQ, TAIL, 2, HEADS, HD)
    prompt = prompt_cache.reshape(PROMPT, 2, HEADS, HD)
    fresh = new_cache.reshape(REQ, FRESH, 2, HEADS, HD)
    queries = query.reshape(REQ, FRESH, HEADS, HD)
    prompt_ok = jnp.arange(PROMPT, dtype=jnp.int32) < prompt_length
    causal = jnp.arange(FRESH, dtype=jnp.int32)[None, :] <= jnp.arange(FRESH, dtype=jnp.int32)[:, None]

    def one_request(operands):
        own_queries, own_tail, own_fresh, own_length = operands
        keyvals = jnp.concatenate([prompt, own_tail, own_fresh], axis=0)
        tail_ok = jnp.arange(TAIL, dtype=jnp.int32) < own_length
        allowed = jnp.concatenate([jnp.broadcast_to(prompt_ok[None, :], (FRESH, PROMPT)), jnp.broadcast_to(tail_ok[None, :], (FRESH, TAIL)), causal], axis=1)

        def one_head(head_operands):
            head_query, head_keys, head_values = head_operands
            return attend_head(head_query, head_keys, head_values, allowed)
        mixed = lax.map(one_head, (own_queries.transpose(1, 0, 2), keyvals[:, 0].transpose(1, 0, 2), keyvals[:, 1].transpose(1, 0, 2)))
        return mixed.transpose(1, 0, 2).reshape(FRESH, HEADS * HD)
    attended = lax.map(one_request, (queries, tails, fresh, tail_len)).reshape(TOKENS, HEADS * HD)
    summed = jnp.dot(attended, w_out, preferred_element_type=jnp.float32)
    hidden_out = (hidden_in.astype(jnp.float32) + summed).astype(jnp.bfloat16)
    return (hidden_out, new_cache)
```

```python
import functools

import jax
import jax.numpy as jnp
from jax import lax
from jax.experimental import pallas as pl
from jax.experimental.pallas import tpu as pltpu
from jax.sharding import PartitionSpec as P

HD = 128
REQ = 8
ROWS = 256
COLS = 256
TPN = 8
KEYS = 1536
NEG = -1e30
SCALE = HD**-0.5 * 1.4426950408889634
MESH = pl.DeviceIdType.MESH


def flip(v, d):
    low = (v % 2 + d % 2) % 2
    high = (v // 2 + d // 2) % 2
    return low + 2 * high


def slot_offsets(i):
    e = i // 4
    r = (i - 3 * e) % 4
    d = r + r // 2 - 2 * (r // 3)
    return d, e


def mix(parts, stats):
    top = functools.reduce(jnp.maximum, [s[0:2] for s in stats])
    raw = [s[2:4] * jnp.exp2(s[0:2] - top) for s in stats]
    total = sum(raw)
    weights = [w / total for w in raw]
    pad = jnp.zeros((128 - 2 * len(stats), ROWS), jnp.float32)
    columns = jnp.concatenate(weights + [pad], axis=0).T
    heads = []
    for h in range(2):
        lanes = slice(h * HD, (h + 1) * HD)
        heads.append(
            sum(
                columns[:, 2 * j + h : 2 * j + h + 1] * part[:, lanes].astype(jnp.float32)
                for j, part in enumerate(parts)
            )
        )
    return jnp.concatenate(heads, axis=1), top, total


def kernel(
    shared_ref, tail_len_ref, table_ref, hid, wq_hbm, wkv_hbm, wo_hbm, prompt, tail_hbm, cos_ref,
    sin_ref, out_ref, nc_ref,
    hbuf, wq, wkv, wo, kv, bias, qbuf, obuf, sbuf, obuf_in, sbuf_in, zo, zs, zo_in, zs_in,
    pair_out, pair_in, acc, rs_out, rs_in,
    lsem, p_send, p_recv, h_send, h_recv, g_send, g_recv, q_send, q_recv, o_send, o_recv,
    s_send, s_recv, w_send, w_recv, r_send, r_recv,
):
    s = lax.axis_index("seq")
    t = lax.axis_index("tp")
    y, x, zh = s // 8, (s // 2) % 4, s % 2
    zl, c = t // 2, t % 2
    member = s % 8
    pair = (s, zl * 2 + 1 - c)
    zpeer = (y * 8 + x * 2 + 1 - zh, t)

    def tp_peer(d):
        return (s, flip(zl, d) * 2 + c)

    def x_peer(d):
        return (y * 8 + flip(x, d) * 2 + zh, t)

    def y_peer(d):
        return (((y + d) % 8) * 8 + x * 2 + zh, t)

    def remote(src, dst, send, recv, device):
        return pltpu.make_async_remote_copy(
            src_ref=src, dst_ref=dst, send_sem=send, recv_sem=recv, device_id=device,
            device_id_type=MESH,
        )

    local = [
        pltpu.make_async_copy(wq_hbm, wq, lsem.at[0]),
        pltpu.make_async_copy(wkv_hbm, wkv, lsem.at[1]),
        pltpu.make_async_copy(wo_hbm, wo, lsem.at[2]),
        pltpu.make_async_copy(tail_hbm, kv.at[pl.ds(256, 256), :], lsem.at[3]),
    ]
    for copy in local:
        copy.start()

    barrier = pltpu.get_barrier_semaphore()
    peers = [pair, zpeer]
    peers += [tp_peer(d) for d in (1, 2, 3)]
    peers += [x_peer(d) for d in (1, 2, 3)]
    peers += [y_peer(d) for d in range(1, 8)]
    for peer in peers:
        pl.semaphore_signal(barrier, inc=1, device_id=peer, device_id_type=MESH)
    pl.semaphore_wait(barrier, len(peers))

    h_copies = {}
    for d in (3, 2, 1):
        h_copies[d] = remote(hid, hbuf.at[t], h_send.at[d], h_recv.at[d], tp_peer(d))
        h_copies[d].start()
    h_copies[0] = remote(hid, hbuf.at[t], h_send.at[0], h_recv.at[0], pair)
    h_copies[0].start()
    p_copies = []
    for d in (4, 3, 5, 2, 6, 1, 7):
        copy = remote(
            prompt, kv.at[pl.ds(512 + d * 128, 128), :], p_send.at[d], p_recv.at[d], y_peer(d)
        )
        copy.start()
        p_copies.append(copy)

    hbuf[t] = hid[...]
    kv[pl.ds(512, 128), :] = prompt[...]
    own_tail = tail_len_ref[y]
    shared = shared_ref[0]
    lane = lax.broadcasted_iota(jnp.int32, (8, 128), 1)
    for k in range(2):
        block = jnp.int32(0)
        for j in range(16):
            block += jnp.where(table_ref[y, j] == s * 2 + k, jnp.int32(j), jnp.int32(0))
        bias[:, k * 128 : (k + 1) * 128] = jnp.where(block * 128 + lane < own_tail, 0.0, NEG)
    for d in range(8):
        start = (((y + 8 - d) % 8) * 8 + x * 2 + zh) * 128
        bias[:, 256 + d * 128 : 384 + d * 128] = jnp.where(start + lane < shared, 0.0, NEG)

    g_copies = []
    for d in (1, 2, 3):
        h_copies[d].wait_recv()
        index = flip(zl, d) * 2 + c
        copy = remote(hbuf.at[index], hbuf.at[index], g_send.at[d], g_recv.at[d], pair)
        copy.start()
        g_copies.append(copy)
    h_copies[0].wait_recv()
    for copy in g_copies:
        copy.wait_recv()

    total = functools.reduce(
        jnp.add, [hbuf[j].astype(jnp.float32) for j in range(TPN)]
    )
    mean = jnp.sum(total, axis=1, keepdims=True) * (1.0 / (TPN * COLS))
    square = jnp.zeros((ROWS, COLS), jnp.float32)
    for j in range(TPN):
        centred = hbuf[j].astype(jnp.float32) - mean
        square += centred * centred
    spread = jnp.sum(square, axis=1, keepdims=True) * (1.0 / (TPN * COLS))
    factor = lax.rsqrt(spread + 1e-05)
    local[0].wait()
    local[1].wait()
    query = jnp.zeros((ROWS, COLS), jnp.float32)
    keyval = jnp.zeros((ROWS, 2 * COLS), jnp.float32)
    for j in range(TPN):
        normed = ((hbuf[j].astype(jnp.float32) - mean) * factor).astype(jnp.bfloat16)
        rows = pl.ds(j * COLS, COLS)
        query += jnp.dot(normed, wq[rows, :], preferred_element_type=jnp.float32)
        keyval += jnp.dot(normed, wkv[rows, :], preferred_element_type=jnp.float32)
    cosine, sine = cos_ref[...], sin_ref[...]

    def rotated(vectors):
        return (vectors * cosine + pltpu.roll(vectors, HD // 2, 1) * sine).astype(jnp.bfloat16)

    for h in range(2):
        lanes = slice(h * HD, (h + 1) * HD)
        qbuf[0, :, lanes] = rotated(query[:, lanes])
    q_copies = {7: remote(qbuf.at[0], qbuf.at[7], q_send.at[7], q_recv.at[7], zpeer)}
    q_copies[7].start()
    for i in (1, 2, 3):
        d, _ = slot_offsets(i)
        q_copies[i] = remote(qbuf.at[0], qbuf.at[i], q_send.at[i], q_recv.at[i], x_peer(d))
        q_copies[i].start()
    for i in (4, 5, 6):
        d, _ = slot_offsets(i)
        q_copies[i] = remote(qbuf.at[7], qbuf.at[i], q_send.at[i], q_recv.at[i], x_peer(d))
    for h in range(2):
        lanes = slice(h * HD, (h + 1) * HD)
        new_key = rotated(keyval[:, lanes])
        kv[pl.ds(0, ROWS), lanes] = new_key
        nc_ref[:, lanes] = new_key
    new_value = keyval[:, COLS:].astype(jnp.bfloat16)
    kv[pl.ds(0, ROWS), COLS:] = new_value
    nc_ref[:, COLS:] = new_value
    local[3].wait()
    for copy in p_copies:
        copy.wait_recv()

    def block(i, carry):
        d, e = slot_offsets(i)
        other = flip(x, d) * 2 + (zh + e) % 2

        @pl.when(i == 2)
        def _():
            q_copies[7].wait_recv()
            for k in (4, 5, 6):
                q_copies[k].start()

        @pl.when((i > 0) & (i < 7))
        def _():
            remote(qbuf.at[0], qbuf.at[i], q_send.at[i], q_recv.at[i], x_peer(d)).wait_recv()

        column = lax.broadcasted_iota(jnp.int32, (ROWS, ROWS), 1)
        row = lax.broadcasted_iota(jnp.int32, (ROWS, ROWS), 0)
        causal = column - row <= (other - member) * ROWS
        tops, totals = [], []
        for h in range(2):
            lanes = slice(h * HD, (h + 1) * HD)
            q = qbuf[i, :, lanes]
            scores = lax.dot_general(
                q, kv[:, lanes], (((1,), (1,)), ((), ())), preferred_element_type=jnp.float32
            ) * SCALE
            fresh = jnp.where(causal, scores[:, :ROWS], NEG)
            cached = scores[:, ROWS:] + bias[0:1, :]
            top = jnp.maximum(
                jnp.max(fresh, axis=1, keepdims=True), jnp.max(cached, axis=1, keepdims=True)
            )
            fresh = jnp.exp2(fresh - top)
            cached = jnp.exp2(cached - top)
            total = jnp.sum(fresh, axis=1, keepdims=True) + jnp.sum(cached, axis=1, keepdims=True)
            mixed = jnp.dot(
                fresh.astype(jnp.bfloat16), kv[0:ROWS, COLS + h * HD : COLS + (h + 1) * HD],
                preferred_element_type=jnp.float32,
            ) + jnp.dot(
                cached.astype(jnp.bfloat16), kv[ROWS:KEYS, COLS + h * HD : COLS + (h + 1) * HD],
                preferred_element_type=jnp.float32,
            )
            obuf[i, :, lanes] = (mixed / total).astype(jnp.bfloat16)
            tops.append(top)
            totals.append(total)
        place = lax.broadcasted_iota(jnp.int32, (ROWS, 128), 1)
        packed = jnp.where(
            place == 0,
            tops[0],
            jnp.where(place == 1, tops[1], jnp.where(place == 2, totals[0], totals[1])),
        )
        sbuf[i] = packed.T[0:8]

        @pl.when((i > 0) & (i < 7))
        def _():
            remote(sbuf.at[i], sbuf_in.at[i], s_send.at[i], s_recv.at[i], x_peer(d)).start()
            remote(obuf.at[i], obuf_in.at[i], o_send.at[i], o_recv.at[i], x_peer(d)).start()

        return carry

    lax.fori_loop(0, 8, block, 0)

    def returned(i):
        d, _ = slot_offsets(i)
        return (
            remote(sbuf.at[i], sbuf_in.at[i], s_send.at[i], s_recv.at[i], x_peer(d)),
            remote(obuf.at[i], obuf_in.at[i], o_send.at[i], o_recv.at[i], x_peer(d)),
        )

    def joined(own, others):
        for i in others:
            for copy in returned(i):
                copy.wait_recv()
        return mix(
            [obuf[own]] + [obuf_in[i] for i in others], [sbuf[own]] + [sbuf_in[i] for i in others]
        )

    mixed, top, total = joined(7, (4, 5, 6))
    zo[...] = mixed.astype(jnp.bfloat16)
    zs[...] = jnp.concatenate([top, total, top, total], axis=0)
    z_copies = [
        remote(zs, zs_in, s_send.at[7], s_recv.at[7], zpeer),
        remote(zo, zo_in, o_send.at[7], o_recv.at[7], zpeer),
    ]
    for copy in z_copies:
        copy.start()
    mixed, top, total = joined(0, (1, 2, 3))
    for copy in z_copies:
        copy.wait_recv()
    mixed, _, _ = mix(
        [mixed, zo_in[...]], [jnp.concatenate([top, total], axis=0), zs_in[...]]
    )
    attended = mixed.astype(jnp.bfloat16)

    local[2].wait()

    def share(d, core):
        start = pl.multiple_of((flip(zl, d) * 2 + core) * COLS, COLS)
        return jnp.dot(attended, wo[:, pl.ds(start, COLS)], preferred_element_type=jnp.float32)

    pair_copies = {}
    for d in (3, 2, 1, 0):
        pair_out[d] = share(d, 1 - c).astype(jnp.bfloat16)
        pair_copies[d] = remote(pair_out.at[d], pair_in.at[d], w_send.at[d], w_recv.at[d], pair)
        pair_copies[d].start()
    for d in (3, 2, 1, 0):
        acc[d] = share(d, c)
    r_copies = {}
    for d in (3, 2, 1):
        pair_copies[d].wait_recv()
        rs_out[d] = (acc[d] + pair_in[d].astype(jnp.float32)).astype(jnp.bfloat16)
        r_copies[d] = remote(rs_out.at[d], rs_in.at[d], r_send.at[d], r_recv.at[d], tp_peer(d))
        r_copies[d].start()
    pair_copies[0].wait_recv()
    summed = hid[...].astype(jnp.float32) + acc[0] + pair_in[0].astype(jnp.float32)
    for d in (1, 2, 3):
        r_copies[d].wait_recv()
        summed += rs_in[d].astype(jnp.float32)
    out_ref[...] = summed.astype(jnp.bfloat16)

    for copies in (h_copies, q_copies, pair_copies, r_copies):
        for copy in copies.values():
            copy.wait_send()
    for copy in p_copies + g_copies + z_copies:
        copy.wait_send()
    for i in range(1, 7):
        for copy in returned(i):
            copy.wait_send()


def local(
    hidden_in, w_query, w_keyval, w_out, prompt_cache, tail_cache, tail_table, tail_len, shared_len
):
    s = lax.axis_index("seq")
    half = HD // 2
    positions = (
        shared_len[0]
        + lax.dynamic_index_in_dim(tail_len, s // REQ, 0, keepdims=False)
        + (s % REQ) * ROWS
        + jnp.arange(ROWS, dtype=jnp.int32)
    )
    freqs = 10000.0 ** (-jnp.arange(half, dtype=jnp.float32) / half)
    angles = positions.astype(jnp.float32)[:, None] * freqs
    cosine, sine = jnp.cos(angles), jnp.sin(angles)
    cosine = jnp.concatenate([cosine, cosine], axis=1)
    sine = jnp.concatenate([-sine, sine], axis=1)
    vmem = pl.BlockSpec(memory_space=pltpu.VMEM)
    smem = pl.BlockSpec(memory_space=pltpu.SMEM)
    anywhere = pl.BlockSpec(memory_space=pl.ANY)
    bf16, f32 = jnp.bfloat16, jnp.float32
    dma = pltpu.SemaphoreType.DMA
    block = (ROWS, COLS)
    out, cache = pl.pallas_call(
        kernel,
        out_shape=(
            jax.ShapeDtypeStruct(block, bf16),
            jax.ShapeDtypeStruct((ROWS, 2 * COLS), bf16),
        ),
        in_specs=[smem, smem, smem, vmem, anywhere, anywhere, anywhere, vmem, anywhere, vmem, vmem],
        out_specs=(vmem, vmem),
        scratch_shapes=[
            pltpu.VMEM((TPN,) + block, bf16),
            pltpu.VMEM((TPN * COLS, COLS), bf16),
            pltpu.VMEM((TPN * COLS, 2 * COLS), bf16),
            pltpu.VMEM((COLS, TPN * COLS), bf16),
            pltpu.VMEM((KEYS, 2 * COLS), bf16),
            pltpu.VMEM((8, KEYS - ROWS), f32),
            pltpu.VMEM((8,) + block, bf16),
            pltpu.VMEM((8,) + block, bf16),
            pltpu.VMEM((8, 8, ROWS), f32),
            pltpu.VMEM((8,) + block, bf16),
            pltpu.VMEM((8, 8, ROWS), f32),
            pltpu.VMEM(block, bf16),
            pltpu.VMEM((8, ROWS), f32),
            pltpu.VMEM(block, bf16),
            pltpu.VMEM((8, ROWS), f32),
            pltpu.VMEM((4,) + block, bf16),
            pltpu.VMEM((4,) + block, bf16),
            pltpu.VMEM((4,) + block, f32),
            pltpu.VMEM((4,) + block, bf16),
            pltpu.VMEM((4,) + block, bf16),
            dma((4,)),
            dma((8,)), dma((8,)),
            dma((4,)), dma((4,)),
            dma((4,)), dma((4,)),
            dma((8,)), dma((8,)),
            dma((8,)), dma((8,)),
            dma((8,)), dma((8,)),
            dma((4,)), dma((4,)),
            dma((4,)), dma((4,)),
        ],
        compiler_params=pltpu.CompilerParams(collective_id=0, has_side_effects=True),
    )(
        shared_len,
        tail_len,
        tail_table,
        hidden_in,
        w_query,
        w_keyval.reshape(TPN * COLS, 2 * COLS),
        w_out,
        prompt_cache.reshape(128, 2 * COLS),
        tail_cache.reshape(ROWS, 2 * COLS),
        cosine,
        sine,
    )
    return (out, cache.reshape(ROWS, 2, COLS))


def solution(mesh):
    return jax.shard_map(
        local,
        mesh=mesh,
        in_specs=(
            P("seq", "tp"),
            P(None, "tp"),
            P(None, None, "tp"),
            P("tp", None),
            P("seq", None, "tp"),
            P("seq", None, None, "tp"),
            P(),
            P(),
            P(),
        ),
        out_specs=(P("seq", "tp"), P("seq", None, "tp")),
        check_vma=False,
    )
```

```python
import functools

import jax
import jax.numpy as jnp
import numpy as np
from jax import lax
from jax.experimental import pallas as pl
from jax.experimental.pallas import tpu as pltpu
from jax.sharding import PartitionSpec as P

HD = 128
REQ = 8
ROWS = 256
COLS = 256
TPN = 8
KEYS = 1536
NEG = -1e30
SCALE = HD**-0.5 * 1.4426950408889634
MESH = pl.DeviceIdType.MESH


def flip(v, d):
    low = (v % 2 + d % 2) % 2
    high = (v // 2 + d // 2) % 2
    return low + 2 * high


def slot_offsets(i):
    e = i // 4
    r = (i - 3 * e) % 4
    d = r + r // 2 - 2 * (r // 3)
    return d, e


def mix(parts, stats):
    top = functools.reduce(jnp.maximum, [s[0:2] for s in stats])
    raw = [s[2:4] * jnp.exp2(s[0:2] - top) for s in stats]
    total = sum(raw)
    weights = [w / total for w in raw]
    pad = jnp.zeros((128 - 2 * len(stats), ROWS), jnp.float32)
    columns = jnp.concatenate(weights + [pad], axis=0).T
    heads = []
    for h in range(2):
        lanes = slice(h * HD, (h + 1) * HD)
        heads.append(
            sum(
                columns[:, 2 * j + h : 2 * j + h + 1] * part[:, lanes].astype(jnp.float32)
                for j, part in enumerate(parts)
            )
        )
    return jnp.concatenate(heads, axis=1), top, total


def kernel(
    shared_ref, tail_len_ref, table_ref, hid, wq_hbm, wkv_hbm, wo_hbm, prompt, tail_hbm,
    freq_ref, out_ref, nc_ref,
    hbuf, wq, wkv_raw, wkv, wo, tail_raw, kv, bias, qbuf, obuf, sbuf, obuf_in, sbuf_in, zo, zs, zo_in, zs_in,
    pair_out, pair_in, acc, rs_out, rs_in,
    lsem, p_send, p_recv, h_send, h_recv, g_send, g_recv, q_send, q_recv, o_send, o_recv,
    s_send, s_recv, w_send, w_recv, r_send, r_recv,
):
    s = lax.axis_index("seq")
    t = lax.axis_index("tp")
    y, x, zh = s // 8, (s // 2) % 4, s % 2
    zl, c = t // 2, t % 2
    member = s % 8
    pair = (s, zl * 2 + 1 - c)
    zpeer = (y * 8 + x * 2 + 1 - zh, t)

    def tp_peer(d):
        return (s, flip(zl, d) * 2 + c)

    def x_peer(d):
        return (y * 8 + flip(x, d) * 2 + zh, t)

    def y_peer(d):
        return (((y + d) % 8) * 8 + x * 2 + zh, t)

    def remote(src, dst, send, recv, device):
        return pltpu.make_async_remote_copy(
            src_ref=src, dst_ref=dst, send_sem=send, recv_sem=recv, device_id=device,
            device_id_type=MESH,
        )

    local = [
        pltpu.make_async_copy(wq_hbm, wq, lsem.at[0]),
        pltpu.make_async_copy(wkv_hbm, wkv_raw, lsem.at[1]),
        pltpu.make_async_copy(wo_hbm, wo, lsem.at[2]),
        pltpu.make_async_copy(tail_hbm, tail_raw, lsem.at[3]),
    ]
    for copy in local:
        copy.start()

    kv[pl.ds(512, 128), 0:COLS] = prompt[:, 0, :]
    kv[pl.ds(512, 128), COLS:] = prompt[:, 1, :]

    barrier = pltpu.get_barrier_semaphore()
    peers = [pair, zpeer]
    peers += [tp_peer(d) for d in (1, 2, 3)]
    peers += [x_peer(d) for d in (1, 2, 3)]
    peers += [y_peer(1), y_peer(7)]
    for peer in peers:
        pl.semaphore_signal(barrier, inc=1, device_id=peer, device_id_type=MESH)
    pl.semaphore_wait(barrier, len(peers))

    h_copies = {}
    for d in (3, 2, 1):
        h_copies[d] = remote(hid, hbuf.at[t], h_send.at[d], h_recv.at[d], tp_peer(d))
        h_copies[d].start()
    h_copies[0] = remote(hid, hbuf.at[t], h_send.at[0], h_recv.at[0], pair)
    h_copies[0].start()
    def ring(step):
        first = 64 if step == 4 else 128
        right = remote(
            kv.at[pl.ds(512 + (step - 1) * 128, first), :],
            kv.at[pl.ds(512 + step * 128, first), :],
            p_send.at[step - 1], p_recv.at[step - 1], y_peer(1),
        )
        shift = 128 - first
        left = remote(
            kv.at[pl.ds(512 + (9 - step) % 8 * 128 + shift, first), :],
            kv.at[pl.ds(512 + (8 - step) * 128 + shift, first), :],
            p_send.at[step + 3], p_recv.at[step + 3], y_peer(7),
        )
        return [right, left]

    p_steps = [ring(step) for step in (1, 2, 3, 4)]

    def forward(step):
        if step > 0:
            for copy in p_steps[step - 1]:
                copy.wait_recv()
        if step < 4:
            for copy in p_steps[step]:
                copy.start()

    forward(0)

    hbuf[t] = hid[...]
    own_tail = tail_len_ref[y]
    shared = shared_ref[0]
    lane = lax.broadcasted_iota(jnp.int32, (8, 128), 1)
    for k in range(2):
        block = jnp.int32(0)
        for j in range(16):
            block += jnp.where(table_ref[y, j] == s * 2 + k, jnp.int32(j), jnp.int32(0))
        bias[:, k * 128 : (k + 1) * 128] = jnp.where(block * 128 + lane < own_tail, 0.0, NEG)
    for d in range(8):
        start = (((y + 8 - d) % 8) * 8 + x * 2 + zh) * 128
        bias[:, 256 + d * 128 : 384 + d * 128] = jnp.where(start + lane < shared, 0.0, NEG)

    positions = shared + own_tail + member * ROWS
    positions = positions + lax.broadcasted_iota(jnp.int32, (ROWS, HD), 0)
    angles = positions.astype(jnp.float32) * freq_ref[0:1, :]
    cosine = jnp.cos(angles)
    sine = jnp.sin(angles) * freq_ref[1:2, :]
    local[3].wait()
    kv[pl.ds(256, 256), 0:COLS] = tail_raw[:, 0, :]
    kv[pl.ds(256, 256), COLS:] = tail_raw[:, 1, :]
    local[1].wait()

    def unweave(k, carry):
        rows = pl.ds(pl.multiple_of(k * 256, 256), 256)
        wkv[rows, 0:COLS] = wkv_raw[rows, 0, :]
        wkv[rows, COLS:] = wkv_raw[rows, 1, :]
        return carry

    lax.fori_loop(0, 4, unweave, 0)
    forward(1)
    lax.fori_loop(4, 8, unweave, 0)
    forward(2)

    g_copies = []
    for d in (1, 2, 3):
        h_copies[d].wait_recv()
        index = flip(zl, d) * 2 + c
        copy = remote(hbuf.at[index], hbuf.at[index], g_send.at[d], g_recv.at[d], pair)
        copy.start()
        g_copies.append(copy)
    forward(3)
    h_copies[0].wait_recv()
    for copy in g_copies:
        copy.wait_recv()

    total = functools.reduce(
        jnp.add, [hbuf[j].astype(jnp.float32) for j in range(TPN)]
    )
    mean = jnp.sum(total, axis=1, keepdims=True) * (1.0 / (TPN * COLS))
    square = jnp.zeros((ROWS, COLS), jnp.float32)
    for j in range(TPN):
        centred = hbuf[j].astype(jnp.float32) - mean
        square += centred * centred
    spread = jnp.sum(square, axis=1, keepdims=True) * (1.0 / (TPN * COLS))
    factor = lax.rsqrt(spread + 1e-05)
    local[0].wait()
    query = jnp.zeros((ROWS, COLS), jnp.float32)
    keyval = jnp.zeros((ROWS, 2 * COLS), jnp.float32)
    for j in range(TPN):
        normed = ((hbuf[j].astype(jnp.float32) - mean) * factor).astype(jnp.bfloat16)
        rows = pl.ds(j * COLS, COLS)
        query += jnp.dot(normed, wq[rows, :], preferred_element_type=jnp.float32)
        keyval += jnp.dot(normed, wkv[rows, :], preferred_element_type=jnp.float32)

    def rotated(vectors):
        return (vectors * cosine + pltpu.roll(vectors, HD // 2, 1) * sine).astype(jnp.bfloat16)

    for h in range(2):
        lanes = slice(h * HD, (h + 1) * HD)
        qbuf[0, :, lanes] = rotated(query[:, lanes])
    q_copies = {7: remote(qbuf.at[0], qbuf.at[7], q_send.at[7], q_recv.at[7], zpeer)}
    q_copies[7].start()
    for i in (1, 2, 3):
        d, _ = slot_offsets(i)
        q_copies[i] = remote(qbuf.at[0], qbuf.at[i], q_send.at[i], q_recv.at[i], x_peer(d))
        q_copies[i].start()
    for i in (4, 5, 6):
        d, _ = slot_offsets(i)
        q_copies[i] = remote(qbuf.at[7], qbuf.at[i], q_send.at[i], q_recv.at[i], x_peer(d))
    for h in range(2):
        lanes = slice(h * HD, (h + 1) * HD)
        new_key = rotated(keyval[:, lanes])
        kv[pl.ds(0, ROWS), lanes] = new_key
        nc_ref[:, lanes] = new_key
    new_value = keyval[:, COLS:].astype(jnp.bfloat16)
    kv[pl.ds(0, ROWS), COLS:] = new_value
    nc_ref[:, COLS:] = new_value
    forward(4)

    def block(i, carry):
        d, e = slot_offsets(i)
        other = flip(x, d) * 2 + (zh + e) % 2

        @pl.when(i == 2)
        def _():
            q_copies[7].wait_recv()
            for k in (4, 5, 6):
                q_copies[k].start()

        @pl.when((i > 0) & (i < 7))
        def _():
            remote(qbuf.at[0], qbuf.at[i], q_send.at[i], q_recv.at[i], x_peer(d)).wait_recv()

        column = lax.broadcasted_iota(jnp.int32, (ROWS, ROWS), 1)
        row = lax.broadcasted_iota(jnp.int32, (ROWS, ROWS), 0)
        causal = column - row <= (other - member) * ROWS
        tops, totals = [], []
        for h in range(2):
            lanes = slice(h * HD, (h + 1) * HD)
            q = qbuf[i, :, lanes]
            scores = lax.dot_general(
                q, kv[:, lanes], (((1,), (1,)), ((), ())), preferred_element_type=jnp.float32
            ) * SCALE
            fresh = jnp.where(causal, scores[:, :ROWS], NEG)
            cached = scores[:, ROWS:] + bias[0:1, :]
            top = jnp.maximum(
                jnp.max(fresh, axis=1, keepdims=True), jnp.max(cached, axis=1, keepdims=True)
            )
            fresh = jnp.exp2(fresh - top)
            cached = jnp.exp2(cached - top)
            total = jnp.sum(fresh, axis=1, keepdims=True) + jnp.sum(cached, axis=1, keepdims=True)
            mixed = jnp.dot(
                fresh.astype(jnp.bfloat16), kv[0:ROWS, COLS + h * HD : COLS + (h + 1) * HD],
                preferred_element_type=jnp.float32,
            ) + jnp.dot(
                cached.astype(jnp.bfloat16), kv[ROWS:KEYS, COLS + h * HD : COLS + (h + 1) * HD],
                preferred_element_type=jnp.float32,
            )
            obuf[i, :, lanes] = (mixed / total).astype(jnp.bfloat16)
            tops.append(top)
            totals.append(total)
        place = lax.broadcasted_iota(jnp.int32, (ROWS, 128), 1)
        packed = jnp.where(
            place == 0,
            tops[0],
            jnp.where(place == 1, tops[1], jnp.where(place == 2, totals[0], totals[1])),
        )
        sbuf[i] = packed.T[0:8]

        @pl.when((i > 0) & (i < 7))
        def _():
            remote(sbuf.at[i], sbuf_in.at[i], s_send.at[i], s_recv.at[i], x_peer(d)).start()
            remote(obuf.at[i], obuf_in.at[i], o_send.at[i], o_recv.at[i], x_peer(d)).start()

        return carry

    lax.fori_loop(0, 8, block, 0)

    def returned(i):
        d, _ = slot_offsets(i)
        return (
            remote(sbuf.at[i], sbuf_in.at[i], s_send.at[i], s_recv.at[i], x_peer(d)),
            remote(obuf.at[i], obuf_in.at[i], o_send.at[i], o_recv.at[i], x_peer(d)),
        )

    def joined(own, others):
        for i in others:
            for copy in returned(i):
                copy.wait_recv()
        return mix(
            [obuf[own]] + [obuf_in[i] for i in others], [sbuf[own]] + [sbuf_in[i] for i in others]
        )

    mixed, top, total = joined(7, (4, 5, 6))
    zo[...] = mixed.astype(jnp.bfloat16)
    zs[...] = jnp.concatenate([top, total, top, total], axis=0)
    z_copies = [
        remote(zs, zs_in, s_send.at[7], s_recv.at[7], zpeer),
        remote(zo, zo_in, o_send.at[7], o_recv.at[7], zpeer),
    ]
    for copy in z_copies:
        copy.start()
    mixed, top, total = joined(0, (1, 2, 3))
    for copy in z_copies:
        copy.wait_recv()
    mixed, _, _ = mix(
        [mixed, zo_in[...]], [jnp.concatenate([top, total], axis=0), zs_in[...]]
    )
    attended = mixed.astype(jnp.bfloat16)

    local[2].wait()

    def share(d, core):
        start = pl.multiple_of((flip(zl, d) * 2 + core) * COLS, COLS)
        return jnp.dot(attended, wo[:, pl.ds(start, COLS)], preferred_element_type=jnp.float32)

    pair_copies = {}
    for d in (3, 2, 1, 0):
        pair_out[d] = share(d, 1 - c).astype(jnp.bfloat16)
        pair_copies[d] = remote(pair_out.at[d], pair_in.at[d], w_send.at[d], w_recv.at[d], pair)
        pair_copies[d].start()
    for d in (3, 2, 1, 0):
        acc[d] = share(d, c)
    r_copies = {}
    for d in (3, 2, 1):
        pair_copies[d].wait_recv()
        rs_out[d] = (acc[d] + pair_in[d].astype(jnp.float32)).astype(jnp.bfloat16)
        r_copies[d] = remote(rs_out.at[d], rs_in.at[d], r_send.at[d], r_recv.at[d], tp_peer(d))
        r_copies[d].start()
    pair_copies[0].wait_recv()
    summed = hid[...].astype(jnp.float32) + acc[0] + pair_in[0].astype(jnp.float32)
    for d in (1, 2, 3):
        r_copies[d].wait_recv()
        summed += rs_in[d].astype(jnp.float32)
    out_ref[...] = summed.astype(jnp.bfloat16)

    for copies in (h_copies, q_copies, pair_copies, r_copies):
        for copy in copies.values():
            copy.wait_send()
    for copy in sum(p_steps, []) + g_copies + z_copies:
        copy.wait_send()
    for i in range(1, 7):
        for copy in returned(i):
            copy.wait_send()


def local(
    hidden_in, w_query, w_keyval, w_out, prompt_cache, tail_cache, tail_table, tail_len, shared_len
):
    half = HD // 2
    freqs = 10000.0 ** (-np.arange(half, dtype=np.float64) / half)
    table = np.zeros((8, HD), np.float32)
    table[0] = np.concatenate([freqs, freqs])
    table[1] = np.concatenate([-np.ones(half), np.ones(half)])
    vmem = pl.BlockSpec(memory_space=pltpu.VMEM)
    smem = pl.BlockSpec(memory_space=pltpu.SMEM)
    anywhere = pl.BlockSpec(memory_space=pl.ANY)
    bf16, f32 = jnp.bfloat16, jnp.float32
    dma = pltpu.SemaphoreType.DMA
    block = (ROWS, COLS)
    out, cache = pl.pallas_call(
        kernel,
        out_shape=(
            jax.ShapeDtypeStruct(block, bf16),
            jax.ShapeDtypeStruct((ROWS, 2 * COLS), bf16),
        ),
        in_specs=[smem, smem, smem, vmem, anywhere, anywhere, anywhere, vmem, anywhere, vmem],
        out_specs=(vmem, vmem),
        scratch_shapes=[
            pltpu.VMEM((TPN,) + block, bf16),
            pltpu.VMEM((TPN * COLS, COLS), bf16),
            pltpu.VMEM((TPN * COLS, 2, COLS), bf16),
            pltpu.VMEM((TPN * COLS, 2 * COLS), bf16),
            pltpu.VMEM((COLS, TPN * COLS), bf16),
            pltpu.VMEM((ROWS, 2, COLS), bf16),
            pltpu.VMEM((KEYS, 2 * COLS), bf16),
            pltpu.VMEM((8, KEYS - ROWS), f32),
            pltpu.VMEM((8,) + block, bf16),
            pltpu.VMEM((8,) + block, bf16),
            pltpu.VMEM((8, 8, ROWS), f32),
            pltpu.VMEM((8,) + block, bf16),
            pltpu.VMEM((8, 8, ROWS), f32),
            pltpu.VMEM(block, bf16),
            pltpu.VMEM((8, ROWS), f32),
            pltpu.VMEM(block, bf16),
            pltpu.VMEM((8, ROWS), f32),
            pltpu.VMEM((4,) + block, bf16),
            pltpu.VMEM((4,) + block, bf16),
            pltpu.VMEM((4,) + block, f32),
            pltpu.VMEM((4,) + block, bf16),
            pltpu.VMEM((4,) + block, bf16),
            dma((4,)),
            dma((8,)), dma((8,)),
            dma((4,)), dma((4,)),
            dma((4,)), dma((4,)),
            dma((8,)), dma((8,)),
            dma((8,)), dma((8,)),
            dma((8,)), dma((8,)),
            dma((4,)), dma((4,)),
            dma((4,)), dma((4,)),
        ],
        compiler_params=pltpu.CompilerParams(collective_id=0, has_side_effects=True),
    )(
        shared_len,
        tail_len,
        tail_table,
        hidden_in,
        w_query,
        w_keyval,
        w_out,
        prompt_cache,
        tail_cache.reshape(ROWS, 2, COLS),
        jnp.asarray(table),
    )
    return (out, cache.reshape(ROWS, 2, COLS))


def solution(mesh):
    return jax.shard_map(
        local,
        mesh=mesh,
        in_specs=(
            P("seq", "tp"),
            P(None, "tp"),
            P(None, None, "tp"),
            P("tp", None),
            P("seq", None, "tp"),
            P("seq", None, None, "tp"),
            P(),
            P(),
            P(),
        ),
        out_specs=(P("seq", "tp"), P("seq", None, "tp")),
        check_vma=False,
    )
```

```python
import functools

import jax
import jax.numpy as jnp
import numpy as np
from jax import lax
from jax.experimental import pallas as pl
from jax.experimental.pallas import tpu as pltpu
from jax.sharding import PartitionSpec as P

HD = 128
REQ = 8
ROWS = 256
COLS = 256
TPN = 8
KEYS = 1536
NEG = -1e30
SCALE = HD**-0.5 * 1.4426950408889634
MESH = pl.DeviceIdType.MESH


def flip(v, d):
    low = (v % 2 + d % 2) % 2
    high = (v // 2 + d // 2) % 2
    return low + 2 * high


def mix(parts, stats):
    top = functools.reduce(jnp.maximum, [s[0:1] for s in stats])
    raw = [s[1:2] * jnp.exp2(s[0:1] - top) for s in stats]
    total = sum(raw)
    pad = jnp.zeros((128 - len(stats), ROWS), jnp.float32)
    columns = jnp.concatenate([w / total for w in raw] + [pad], axis=0).T
    mixed = sum(columns[:, j : j + 1] * part.astype(jnp.float32) for j, part in enumerate(parts))
    return mixed, top, total


def kernel(
    shared_ref, tail_len_ref, table_ref, hid, wq_hbm, wkv_hbm, wo_hbm, prompt, tail_hbm,
    freq_ref, out_ref, nc_ref,
    hbuf, wq, wkv_raw, wkv, wo, tail_raw, kv, bias, qbuf, obuf, sbuf, obuf_in, sbuf_in, zo, zs, zo_in, zs_in,
    nbuf, wo_in, att, att_in, rs_out, rs_in,
    lsem, p_send, p_recv, h_send, h_recv, g_send, g_recv, q_send, q_recv, o_send, o_recv,
    s_send, s_recv, w_send, w_recv, a_send, a_recv, r_send, r_recv,
):
    s = lax.axis_index("seq")
    t = lax.axis_index("tp")
    y, x, zh = s // 8, (s // 2) % 4, s % 2
    zl, c = t // 2, t % 2
    member = s % 8
    pair = (s, zl * 2 + 1 - c)
    zpeer = (y * 8 + x * 2 + 1 - zh, t)

    def tp_peer(d):
        return (s, flip(zl, d) * 2 + c)

    def x_peer(d):
        return (y * 8 + flip(x, d) * 2 + zh, t)

    def y_peer(d):
        return (((y + d) % 8) * 8 + x * 2 + zh, t)

    def remote(src, dst, send, recv, device):
        return pltpu.make_async_remote_copy(
            src_ref=src, dst_ref=dst, send_sem=send, recv_sem=recv, device_id=device,
            device_id_type=MESH,
        )

    local = [
        pltpu.make_async_copy(wq_hbm, wq, lsem.at[0]),
        pltpu.make_async_copy(wkv_hbm, wkv_raw, lsem.at[1]),
        pltpu.make_async_copy(wo_hbm, wo, lsem.at[2]),
        pltpu.make_async_copy(tail_hbm, tail_raw, lsem.at[3]),
    ]
    for copy in local:
        copy.start()

    kv[pl.ds(512, 128), 0:COLS] = prompt[:, 0, :]
    kv[pl.ds(512, 128), COLS:] = prompt[:, 1, :]

    barrier = pltpu.get_barrier_semaphore()
    peers = [pair, zpeer]
    peers += [tp_peer(d) for d in (1, 2, 3)]
    peers += [x_peer(d) for d in (1, 2, 3)]
    peers += [y_peer(1), y_peer(7)]
    for peer in peers:
        pl.semaphore_signal(barrier, inc=1, device_id=peer, device_id_type=MESH)
    pl.semaphore_wait(barrier, len(peers))

    h_copies = {}
    for d in (3, 2, 1):
        h_copies[d] = remote(hid, hbuf.at[t], h_send.at[d], h_recv.at[d], tp_peer(d))
        h_copies[d].start()
    h_copies[0] = remote(hid, hbuf.at[t], h_send.at[0], h_recv.at[0], pair)
    h_copies[0].start()
    def ring(step):
        first = 64 if step == 4 else 128
        right = remote(
            kv.at[pl.ds(512 + (step - 1) * 128, first), :],
            kv.at[pl.ds(512 + step * 128, first), :],
            p_send.at[step - 1], p_recv.at[step - 1], y_peer(1),
        )
        shift = 128 - first
        left = remote(
            kv.at[pl.ds(512 + (9 - step) % 8 * 128 + shift, first), :],
            kv.at[pl.ds(512 + (8 - step) * 128 + shift, first), :],
            p_send.at[step + 3], p_recv.at[step + 3], y_peer(7),
        )
        return [right, left]

    p_steps = [ring(step) for step in (1, 2, 3, 4)]

    def forward(step):
        if step > 0:
            for copy in p_steps[step - 1]:
                copy.wait_recv()
        if step < 4:
            for copy in p_steps[step]:
                copy.start()

    forward(0)

    hbuf[t] = hid[...]
    own_tail = tail_len_ref[y]
    shared = shared_ref[0]
    lane = lax.broadcasted_iota(jnp.int32, (8, 128), 1)
    for k in range(2):
        block = jnp.int32(0)
        for j in range(16):
            block += jnp.where(table_ref[y, j] == s * 2 + k, jnp.int32(j), jnp.int32(0))
        bias[:, k * 128 : (k + 1) * 128] = jnp.where(block * 128 + lane < own_tail, 0.0, NEG)
    for d in range(8):
        start = (((y + 8 - d) % 8) * 8 + x * 2 + zh) * 128
        bias[:, 256 + d * 128 : 384 + d * 128] = jnp.where(start + lane < shared, 0.0, NEG)

    positions = shared + own_tail + member * ROWS
    positions = positions + lax.broadcasted_iota(jnp.int32, (ROWS, HD), 0)
    angles = positions.astype(jnp.float32) * freq_ref[0:1, :]
    cosine = jnp.cos(angles)
    sine = jnp.sin(angles) * freq_ref[1:2, :]
    local[3].wait()
    kv[pl.ds(256, 256), 0:COLS] = tail_raw[:, 0, :]
    kv[pl.ds(256, 256), COLS:] = tail_raw[:, 1, :]
    local[1].wait()

    def unweave(k, carry):
        rows = pl.ds(pl.multiple_of(k * 256, 256), 256)
        wkv[rows, 0:COLS] = wkv_raw[rows, 0, :]
        wkv[rows, COLS:] = wkv_raw[rows, 1, :]
        return carry

    lax.fori_loop(0, 4, unweave, 0)
    forward(1)
    local[2].wait()
    w_copies = []
    for d in range(4):
        start = pl.multiple_of((flip(zl, d) * 2 + 1 - c) * COLS, COLS)
        w_copies.append(
            remote(wo.at[:, pl.ds(start, COLS)], wo_in.at[d], w_send.at[d], w_recv.at[d], pair)
        )
        w_copies[d].start()
    lax.fori_loop(4, 8, unweave, 0)
    forward(2)

    g_copies = []
    for d in (1, 2, 3):
        h_copies[d].wait_recv()
        index = flip(zl, d) * 2 + c
        copy = remote(hbuf.at[index], hbuf.at[index], g_send.at[d], g_recv.at[d], pair)
        copy.start()
        g_copies.append(copy)
    forward(3)
    h_copies[0].wait_recv()
    for copy in g_copies:
        copy.wait_recv()

    total = functools.reduce(
        jnp.add, [hbuf[j].astype(jnp.float32) for j in range(TPN)]
    )
    mean = jnp.sum(total, axis=1, keepdims=True) * (1.0 / (TPN * COLS))
    square = jnp.zeros((ROWS, COLS), jnp.float32)
    for j in range(TPN):
        centred = hbuf[j].astype(jnp.float32) - mean
        square += centred * centred
    spread = jnp.sum(square, axis=1, keepdims=True) * (1.0 / (TPN * COLS))
    factor = lax.rsqrt(spread + 1e-05)
    local[0].wait()
    query = jnp.zeros((ROWS, COLS), jnp.float32)
    for j in range(TPN):
        normed = ((hbuf[j].astype(jnp.float32) - mean) * factor).astype(jnp.bfloat16)
        nbuf[j] = normed
        query += jnp.dot(
            normed, wq[pl.ds(j * COLS, COLS), :], preferred_element_type=jnp.float32
        )

    def rotated(vectors):
        return (vectors * cosine + pltpu.roll(vectors, HD // 2, 1) * sine).astype(jnp.bfloat16)

    q_copies = {}
    for h in range(2):
        qbuf[h, 0] = rotated(query[:, h * HD : (h + 1) * HD])
        for slot in (4, 1, 3, 2):
            q_copies[h, slot] = remote(
                qbuf.at[h, 0], qbuf.at[h, slot], q_send.at[h, slot], q_recv.at[h, slot],
                zpeer if slot == 4 else x_peer(slot),
            )
            q_copies[h, slot].start()
        for slot in (5, 7, 6):
            q_copies[h, slot] = remote(
                qbuf.at[h, 4], qbuf.at[h, slot], q_send.at[h, slot], q_recv.at[h, slot],
                x_peer(slot - 4),
            )
    keyval = jnp.zeros((ROWS, 2 * COLS), jnp.float32)
    for j in range(TPN):
        keyval += jnp.dot(
            nbuf[j], wkv[pl.ds(j * COLS, COLS), :], preferred_element_type=jnp.float32
        )
    for h in range(2):
        lanes = slice(h * HD, (h + 1) * HD)
        new_key = rotated(keyval[:, lanes])
        kv[pl.ds(0, ROWS), lanes] = new_key
        nc_ref[:, lanes] = new_key
    new_value = keyval[:, COLS:].astype(jnp.bfloat16)
    kv[pl.ds(0, ROWS), COLS:] = new_value
    nc_ref[:, COLS:] = new_value
    forward(4)

    def returned(h, slot, d):
        return (
            remote(
                sbuf.at[h, slot], sbuf_in.at[h, slot], s_send.at[h, slot], s_recv.at[h, slot],
                x_peer(d),
            ),
            remote(
                obuf.at[h, slot], obuf_in.at[h, slot], o_send.at[h, slot], o_recv.at[h, slot],
                x_peer(d),
            ),
        )

    def attend(h, slot, d, e):
        other = flip(x, d) * 2 + (zh + e) % 2
        column = lax.broadcasted_iota(jnp.int32, (ROWS, ROWS), 1)
        row = lax.broadcasted_iota(jnp.int32, (ROWS, ROWS), 0)
        causal = column - row <= (other - member) * ROWS
        values = slice(COLS + h * HD, COLS + (h + 1) * HD)
        scores = lax.dot_general(
            qbuf[h, slot], kv[:, h * HD : (h + 1) * HD], (((1,), (1,)), ((), ())),
            preferred_element_type=jnp.float32,
        ) * SCALE
        fresh = jnp.where(causal, scores[:, :ROWS], NEG)
        cached = scores[:, ROWS:] + bias[0:1, :]
        top = jnp.maximum(
            jnp.max(fresh, axis=1, keepdims=True), jnp.max(cached, axis=1, keepdims=True)
        )
        fresh = jnp.exp2(fresh - top)
        cached = jnp.exp2(cached - top)
        total = jnp.sum(fresh, axis=1, keepdims=True) + jnp.sum(cached, axis=1, keepdims=True)
        mixed = jnp.dot(
            fresh.astype(jnp.bfloat16), kv[0:ROWS, values], preferred_element_type=jnp.float32
        ) + jnp.dot(
            cached.astype(jnp.bfloat16), kv[ROWS:KEYS, values], preferred_element_type=jnp.float32
        )
        obuf[h, slot] = (mixed / total).astype(jnp.bfloat16)
        place = lax.broadcasted_iota(jnp.int32, (ROWS, 128), 1)
        sbuf[h, slot] = jnp.where(place == 0, top, total).T[0:8]

    def arrive(h, slot, d):
        remote(
            qbuf.at[h, 0], qbuf.at[h, slot], q_send.at[h, slot], q_recv.at[h, slot], x_peer(d)
        ).wait_recv()

    def give(h, slot, d):
        for copy in returned(h, slot, d):
            copy.start()

    def near(h, first, last):
        def body(i, carry):
            d = i + i // 2 - 2 * (i // 3)

            @pl.when(i > 0)
            def _():
                arrive(h, d, d)

            attend(h, d, d, 0)

            @pl.when(i > 0)
            def _():
                give(h, d, d)

            return carry

        lax.fori_loop(first, last, body, 0)

    def far(h):
        def body(i, carry):
            d = i + i // 2 - 2 * (i // 3)
            arrive(h, 4 + d, d)
            attend(h, 4 + d, d, 1)
            give(h, 4 + d, d)
            return carry

        lax.fori_loop(1, 4, body, 0)

    def relay(h):
        q_copies[h, 4].wait_recv()
        for slot in (5, 7, 6):
            q_copies[h, slot].start()

    def joined(h, own):
        others = [own + d for d in (1, 2, 3)]
        for slot in others:
            for copy in returned(h, slot, slot - own):
                copy.wait_recv()
        return mix(
            [obuf[h, own]] + [obuf_in[h, slot] for slot in others],
            [sbuf[h, own]] + [sbuf_in[h, slot] for slot in others],
        )

    z_copies = []

    def across(h):
        mixed, top, total = joined(h, 4)
        zo[h] = mixed.astype(jnp.bfloat16)
        zs[h] = jnp.concatenate([top, total] * 4, axis=0)
        z_copies.append(remote(zs.at[h], zs_in.at[h], s_send.at[h, 4], s_recv.at[h, 4], zpeer))
        z_copies.append(remote(zo.at[h], zo_in.at[h], o_send.at[h, 4], o_recv.at[h, 4], zpeer))
        for copy in z_copies[-2:]:
            copy.start()

    near(0, 0, 4)
    near(1, 0, 2)
    relay(0)
    near(1, 2, 4)
    relay(1)
    attend(0, 4, 0, 1)
    far(0)
    attend(1, 4, 0, 1)
    across(0)
    far(1)
    across(1)
    a_copies = []
    for h in range(2):
        mixed, top, total = joined(h, 0)
        for copy in z_copies[2 * h : 2 * h + 2]:
            copy.wait_recv()
        mixed, _, _ = mix(
            [mixed, zo_in[h]], [jnp.concatenate([top, total] * 4, axis=0), zs_in[h]]
        )
        att[h] = mixed.astype(jnp.bfloat16)
        a_copies.append(remote(att.at[h], att_in.at[h], a_send.at[h], a_recv.at[h], pair))
        a_copies[h].start()

    own = jnp.concatenate([att[0], att[1]], axis=1)
    for copy in w_copies + a_copies:
        copy.wait_recv()
    partner = jnp.concatenate([att_in[0], att_in[1]], axis=1)

    def share(d):
        start = pl.multiple_of((flip(zl, d) * 2 + c) * COLS, COLS)
        return jnp.dot(
            own, wo[:, pl.ds(start, COLS)], preferred_element_type=jnp.float32
        ) + jnp.dot(partner, wo_in[d], preferred_element_type=jnp.float32)

    r_copies = {}
    for d in (3, 2, 1):
        rs_out[d] = share(d).astype(jnp.bfloat16)
        r_copies[d] = remote(rs_out.at[d], rs_in.at[d], r_send.at[d], r_recv.at[d], tp_peer(d))
        r_copies[d].start()
    summed = hid[...].astype(jnp.float32) + share(0)
    for d in (1, 2, 3):
        r_copies[d].wait_recv()
        summed += rs_in[d].astype(jnp.float32)
    out_ref[...] = summed.astype(jnp.bfloat16)

    for copies in (h_copies, q_copies, r_copies):
        for copy in copies.values():
            copy.wait_send()
    for copy in sum(p_steps, []) + g_copies + z_copies + w_copies + a_copies:
        copy.wait_send()
    for h in range(2):
        for slot in (1, 2, 3, 5, 6, 7):
            for copy in returned(h, slot, slot % 4):
                copy.wait_send()


def local(
    hidden_in, w_query, w_keyval, w_out, prompt_cache, tail_cache, tail_table, tail_len, shared_len
):
    half = HD // 2
    freqs = 10000.0 ** (-np.arange(half, dtype=np.float64) / half)
    table = np.zeros((8, HD), np.float32)
    table[0] = np.concatenate([freqs, freqs])
    table[1] = np.concatenate([-np.ones(half), np.ones(half)])
    vmem = pl.BlockSpec(memory_space=pltpu.VMEM)
    smem = pl.BlockSpec(memory_space=pltpu.SMEM)
    anywhere = pl.BlockSpec(memory_space=pl.ANY)
    bf16, f32 = jnp.bfloat16, jnp.float32
    dma = pltpu.SemaphoreType.DMA
    block = (ROWS, COLS)
    out, cache = pl.pallas_call(
        kernel,
        out_shape=(
            jax.ShapeDtypeStruct(block, bf16),
            jax.ShapeDtypeStruct((ROWS, 2 * COLS), bf16),
        ),
        in_specs=[smem, smem, smem, vmem, anywhere, anywhere, anywhere, vmem, anywhere, vmem],
        out_specs=(vmem, vmem),
        scratch_shapes=[
            pltpu.VMEM((TPN,) + block, bf16),
            pltpu.VMEM((TPN * COLS, COLS), bf16),
            pltpu.VMEM((TPN * COLS, 2, COLS), bf16),
            pltpu.VMEM((TPN * COLS, 2 * COLS), bf16),
            pltpu.VMEM((COLS, TPN * COLS), bf16),
            pltpu.VMEM((ROWS, 2, COLS), bf16),
            pltpu.VMEM((KEYS, 2 * COLS), bf16),
            pltpu.VMEM((8, KEYS - ROWS), f32),
            pltpu.VMEM((2, 8, ROWS, HD), bf16),
            pltpu.VMEM((2, 8, ROWS, HD), bf16),
            pltpu.VMEM((2, 8, 8, ROWS), f32),
            pltpu.VMEM((2, 8, ROWS, HD), bf16),
            pltpu.VMEM((2, 8, 8, ROWS), f32),
            pltpu.VMEM((2, ROWS, HD), bf16),
            pltpu.VMEM((2, 8, ROWS), f32),
            pltpu.VMEM((2, ROWS, HD), bf16),
            pltpu.VMEM((2, 8, ROWS), f32),
            pltpu.VMEM((TPN,) + block, bf16),
            pltpu.VMEM((4,) + block, bf16),
            pltpu.VMEM((2, ROWS, HD), bf16),
            pltpu.VMEM((2, ROWS, HD), bf16),
            pltpu.VMEM((4,) + block, bf16),
            pltpu.VMEM((4,) + block, bf16),
            dma((4,)),
            dma((8,)), dma((8,)),
            dma((4,)), dma((4,)),
            dma((4,)), dma((4,)),
            dma((2, 8)), dma((2, 8)),
            dma((2, 8)), dma((2, 8)),
            dma((2, 8)), dma((2, 8)),
            dma((4,)), dma((4,)),
            dma((2,)), dma((2,)),
            dma((4,)), dma((4,)),
        ],
        compiler_params=pltpu.CompilerParams(collective_id=0, has_side_effects=True),
    )(
        shared_len,
        tail_len,
        tail_table,
        hidden_in,
        w_query,
        w_keyval,
        w_out,
        prompt_cache,
        tail_cache.reshape(ROWS, 2, COLS),
        jnp.asarray(table),
    )
    return (out, cache.reshape(ROWS, 2, COLS))


def solution(mesh):
    return jax.shard_map(
        local,
        mesh=mesh,
        in_specs=(
            P("seq", "tp"),
            P(None, "tp"),
            P(None, None, "tp"),
            P("tp", None),
            P("seq", None, "tp"),
            P("seq", None, None, "tp"),
            P(),
            P(),
            P(),
        ),
        out_specs=(P("seq", "tp"), P("seq", None, "tp")),
        check_vma=False,
    )
```

```python
import functools

import jax
import jax.numpy as jnp
import numpy as np
from jax import lax
from jax.experimental import pallas as pl
from jax.experimental.pallas import tpu as pltpu
from jax.sharding import PartitionSpec as P

HD = 128
REQ = 8
ROWS = 256
COLS = 256
TPN = 8
KEYS = 1536
NEG = -1e30
SCALE = HD**-0.5 * 1.4426950408889634
MESH = pl.DeviceIdType.MESH


def flip(v, d):
    low = (v % 2 + d % 2) % 2
    high = (v // 2 + d // 2) % 2
    return low + 2 * high


def mix(parts, stats):
    top = functools.reduce(jnp.maximum, [s[0:1] for s in stats])
    raw = [s[1:2] * jnp.exp2(s[0:1] - top) for s in stats]
    total = sum(raw)
    pad = jnp.zeros((128 - len(stats), ROWS), jnp.float32)
    columns = jnp.concatenate([w / total for w in raw] + [pad], axis=0).T
    mixed = sum(columns[:, j : j + 1] * part.astype(jnp.float32) for j, part in enumerate(parts))
    return mixed, top, total


def kernel(
    shared_ref, tail_len_ref, table_ref, hid, wq_hbm, wkv_hbm, wo_hbm, prompt, tail_hbm,
    freq_ref, out_ref, nc_ref,
    hbuf, wq, wkv_raw, wkv, wo, tail_raw, kv, bias, qbuf, obuf, sbuf, obuf_in, sbuf_in, zo, zs, zo_in, zs_in,
    nbuf, q_hop, o_hop, v_send, v_recv, wo_in, att, att_in, rs_out, rs_in,
    lsem, p_send, p_recv, h_send, h_recv, g_send, g_recv, q_send, q_recv, o_send, o_recv,
    s_send, s_recv, w_send, w_recv, a_send, a_recv, r_send, r_recv,
):
    s = lax.axis_index("seq")
    t = lax.axis_index("tp")
    y, x, zh = s // 8, (s // 2) % 4, s % 2
    zl, c = t // 2, t % 2
    member = s % 8
    pair = (s, zl * 2 + 1 - c)
    zpeer = (y * 8 + x * 2 + 1 - zh, t)

    def tp_peer(d):
        return (s, flip(zl, d) * 2 + c)

    def x_peer(d):
        return (y * 8 + flip(x, d) * 2 + zh, t)

    def y_peer(d):
        return (((y + d) % 8) * 8 + x * 2 + zh, t)

    def z_peer(shift):
        z = (zh * 4 + zl + shift) % 8
        return (y * 8 + x * 2 + z // 4, z % 4 * 2 + c)

    def remote(src, dst, send, recv, device):
        return pltpu.make_async_remote_copy(
            src_ref=src, dst_ref=dst, send_sem=send, recv_sem=recv, device_id=device,
            device_id_type=MESH,
        )

    local = [
        pltpu.make_async_copy(wq_hbm, wq, lsem.at[0]),
        pltpu.make_async_copy(wkv_hbm, wkv_raw, lsem.at[1]),
        pltpu.make_async_copy(wo_hbm, wo, lsem.at[2]),
        pltpu.make_async_copy(tail_hbm, tail_raw, lsem.at[3]),
    ]
    for copy in local:
        copy.start()

    kv[pl.ds(512, 128), 0:COLS] = prompt[:, 0, :]
    kv[pl.ds(512, 128), COLS:] = prompt[:, 1, :]

    barrier = pltpu.get_barrier_semaphore()
    peers = [pair, zpeer]
    peers += [tp_peer(d) for d in (1, 2, 3)]
    peers += [x_peer(d) for d in (1, 2, 3)]
    peers += [y_peer(1), y_peer(7)]
    peers += [z_peer(shift) for shift in (1, 7, 3, 5)]
    for peer in peers:
        pl.semaphore_signal(barrier, inc=1, device_id=peer, device_id_type=MESH)
    pl.semaphore_wait(barrier, len(peers))

    h_copies = {}
    for d in (3, 2, 1):
        h_copies[d] = remote(hid, hbuf.at[t], h_send.at[d], h_recv.at[d], tp_peer(d))
        h_copies[d].start()
    h_copies[0] = remote(hid, hbuf.at[t], h_send.at[0], h_recv.at[0], pair)
    h_copies[0].start()
    def ring(step):
        first = 64 if step == 4 else 128
        right = remote(
            kv.at[pl.ds(512 + (step - 1) * 128, first), :],
            kv.at[pl.ds(512 + step * 128, first), :],
            p_send.at[step - 1], p_recv.at[step - 1], y_peer(1),
        )
        shift = 128 - first
        left = remote(
            kv.at[pl.ds(512 + (9 - step) % 8 * 128 + shift, first), :],
            kv.at[pl.ds(512 + (8 - step) * 128 + shift, first), :],
            p_send.at[step + 3], p_recv.at[step + 3], y_peer(7),
        )
        return [right, left]

    p_steps = [ring(step) for step in (1, 2, 3, 4)]

    def forward(step):
        if step > 0:
            for copy in p_steps[step - 1]:
                copy.wait_recv()
        if step < 4:
            for copy in p_steps[step]:
                copy.start()

    forward(0)

    hbuf[t] = hid[...]
    own_tail = tail_len_ref[y]
    shared = shared_ref[0]
    lane = lax.broadcasted_iota(jnp.int32, (8, 128), 1)
    for k in range(2):
        block = jnp.int32(0)
        for j in range(16):
            block += jnp.where(table_ref[y, j] == s * 2 + k, jnp.int32(j), jnp.int32(0))
        bias[:, k * 128 : (k + 1) * 128] = jnp.where(block * 128 + lane < own_tail, 0.0, NEG)
    for d in range(8):
        start = (((y + 8 - d) % 8) * 8 + x * 2 + zh) * 128
        bias[:, 256 + d * 128 : 384 + d * 128] = jnp.where(start + lane < shared, 0.0, NEG)

    positions = shared + own_tail + member * ROWS
    positions = positions + lax.broadcasted_iota(jnp.int32, (ROWS, HD), 0)
    angles = positions.astype(jnp.float32) * freq_ref[0:1, :]
    cosine = jnp.cos(angles)
    sine = jnp.sin(angles) * freq_ref[1:2, :]
    local[3].wait()
    kv[pl.ds(256, 256), 0:COLS] = tail_raw[:, 0, :]
    kv[pl.ds(256, 256), COLS:] = tail_raw[:, 1, :]
    local[1].wait()

    def unweave(k, carry):
        rows = pl.ds(pl.multiple_of(k * 256, 256), 256)
        wkv[rows, 0:COLS] = wkv_raw[rows, 0, :]
        wkv[rows, COLS:] = wkv_raw[rows, 1, :]
        return carry

    lax.fori_loop(0, 4, unweave, 0)
    forward(1)
    lax.fori_loop(4, 8, unweave, 0)
    forward(2)

    g_copies = []
    for d in (1, 2, 3):
        h_copies[d].wait_recv()
        index = flip(zl, d) * 2 + c
        copy = remote(hbuf.at[index], hbuf.at[index], g_send.at[d], g_recv.at[d], pair)
        copy.start()
        g_copies.append(copy)
    forward(3)
    h_copies[0].wait_recv()
    for copy in g_copies:
        copy.wait_recv()

    total = functools.reduce(
        jnp.add, [hbuf[j].astype(jnp.float32) for j in range(TPN)]
    )
    mean = jnp.sum(total, axis=1, keepdims=True) * (1.0 / (TPN * COLS))
    square = jnp.zeros((ROWS, COLS), jnp.float32)
    for j in range(TPN):
        centred = hbuf[j].astype(jnp.float32) - mean
        square += centred * centred
    spread = jnp.sum(square, axis=1, keepdims=True) * (1.0 / (TPN * COLS))
    factor = lax.rsqrt(spread + 1e-05)
    local[0].wait()
    query = jnp.zeros((ROWS, COLS), jnp.float32)
    for j in range(TPN):
        normed = ((hbuf[j].astype(jnp.float32) - mean) * factor).astype(jnp.bfloat16)
        nbuf[j] = normed
        query += jnp.dot(
            normed, wq[pl.ds(j * COLS, COLS), :], preferred_element_type=jnp.float32
        )

    def rotated(vectors):
        return (vectors * cosine + pltpu.roll(vectors, HD // 2, 1) * sine).astype(jnp.bfloat16)

    q_down = remote(qbuf.at[1, 0], q_hop, v_send.at[0], v_recv.at[0], z_peer(7))
    q_copies = {}
    for h in range(2):
        qbuf[h, 0] = rotated(query[:, h * HD : (h + 1) * HD])
        for slot in (4, 1, 3, 2):
            down = slot == 4 and h == 1
            q_copies[h, slot] = remote(
                q_hop if down else qbuf.at[h, 0],
                qbuf.at[h, slot], q_send.at[h, slot], q_recv.at[h, slot],
                x_peer(slot) if slot < 4 else z_peer(5) if down else zpeer,
            )
            (q_down if down else q_copies[h, slot]).start()
        for slot in (5, 7, 6):
            q_copies[h, slot] = remote(
                qbuf.at[h, 4], qbuf.at[h, slot], q_send.at[h, slot], q_recv.at[h, slot],
                x_peer(slot - 4),
            )
    local[2].wait()
    w_copies = []
    for d in range(4):
        start = pl.multiple_of((flip(zl, d) * 2 + 1 - c) * COLS, COLS)
        w_copies.append(
            remote(wo.at[:, pl.ds(start, COLS)], wo_in.at[d], w_send.at[d], w_recv.at[d], pair)
        )
        w_copies[d].start()
    keyval = jnp.zeros((ROWS, 2 * COLS), jnp.float32)
    for j in range(TPN):
        keyval += jnp.dot(
            nbuf[j], wkv[pl.ds(j * COLS, COLS), :], preferred_element_type=jnp.float32
        )
    q_down.wait_recv()
    q_copies[1, 4].start()
    for h in range(2):
        lanes = slice(h * HD, (h + 1) * HD)
        new_key = rotated(keyval[:, lanes])
        kv[pl.ds(0, ROWS), lanes] = new_key
        nc_ref[:, lanes] = new_key
    new_value = keyval[:, COLS:].astype(jnp.bfloat16)
    kv[pl.ds(0, ROWS), COLS:] = new_value
    nc_ref[:, COLS:] = new_value
    forward(4)

    def returned(h, slot, d):
        return (
            remote(
                sbuf.at[h, slot], sbuf_in.at[h, slot], s_send.at[h, slot], s_recv.at[h, slot],
                x_peer(d),
            ),
            remote(
                obuf.at[h, slot], obuf_in.at[h, slot], o_send.at[h, slot], o_recv.at[h, slot],
                x_peer(d),
            ),
        )

    def attend(h, slot, d, e):
        other = flip(x, d) * 2 + (zh + e) % 2
        column = lax.broadcasted_iota(jnp.int32, (ROWS, ROWS), 1)
        row = lax.broadcasted_iota(jnp.int32, (ROWS, ROWS), 0)
        causal = column - row <= (other - member) * ROWS
        values = slice(COLS + h * HD, COLS + (h + 1) * HD)
        scores = lax.dot_general(
            qbuf[h, slot], kv[:, h * HD : (h + 1) * HD], (((1,), (1,)), ((), ())),
            preferred_element_type=jnp.float32,
        ) * SCALE
        fresh = jnp.where(causal, scores[:, :ROWS], NEG)
        cached = scores[:, ROWS:] + bias[0:1, :]
        top = jnp.maximum(
            jnp.max(fresh, axis=1, keepdims=True), jnp.max(cached, axis=1, keepdims=True)
        )
        fresh = jnp.exp2(fresh - top)
        cached = jnp.exp2(cached - top)
        total = jnp.sum(fresh, axis=1, keepdims=True) + jnp.sum(cached, axis=1, keepdims=True)
        mixed = jnp.dot(
            fresh.astype(jnp.bfloat16), kv[0:ROWS, values], preferred_element_type=jnp.float32
        ) + jnp.dot(
            cached.astype(jnp.bfloat16), kv[ROWS:KEYS, values], preferred_element_type=jnp.float32
        )
        obuf[h, slot] = (mixed / total).astype(jnp.bfloat16)
        place = lax.broadcasted_iota(jnp.int32, (ROWS, 128), 1)
        sbuf[h, slot] = jnp.where(place == 0, top, total).T[0:8]

    def arrive(h, slot, d):
        remote(
            qbuf.at[h, 0], qbuf.at[h, slot], q_send.at[h, slot], q_recv.at[h, slot], x_peer(d)
        ).wait_recv()

    def give(h, slot, d):
        for copy in returned(h, slot, d):
            copy.start()

    def near(h, first, last):
        def body(i, carry):
            d = i + i // 2 - 2 * (i // 3)

            @pl.when(i > 0)
            def _():
                arrive(h, d, d)

            attend(h, d, d, 0)

            @pl.when(i > 0)
            def _():
                give(h, d, d)

            return carry

        lax.fori_loop(first, last, body, 0)

    def far(h):
        def body(i, carry):
            d = i + i // 2 - 2 * (i // 3)
            arrive(h, 4 + d, d)
            attend(h, 4 + d, d, 1)
            give(h, 4 + d, d)
            return carry

        lax.fori_loop(1, 4, body, 0)

    def relay(h):
        q_copies[h, 4].wait_recv()
        for slot in (5, 7, 6):
            q_copies[h, slot].start()

    def joined(h, own):
        others = [own + d for d in (1, 2, 3)]
        for slot in others:
            for copy in returned(h, slot, slot - own):
                copy.wait_recv()
        return mix(
            [obuf[h, own]] + [obuf_in[h, slot] for slot in others],
            [sbuf[h, own]] + [sbuf_in[h, slot] for slot in others],
        )

    z_copies = []
    o_down = remote(zo.at[1], o_hop, v_send.at[1], v_recv.at[1], z_peer(7))

    def across(h):
        mixed, top, total = joined(h, 4)
        zo[h] = mixed.astype(jnp.bfloat16)
        zs[h] = jnp.concatenate([top, total] * 4, axis=0)
        z_copies.append(remote(zs.at[h], zs_in.at[h], s_send.at[h, 4], s_recv.at[h, 4], zpeer))
        z_copies[-1].start()
        if h == 0:
            z_copies.append(
                remote(zo.at[0], zo_in.at[0], o_send.at[0, 4], o_recv.at[0, 4], zpeer)
            )
            z_copies[-1].start()
        else:
            o_down.start()
            z_copies.append(
                remote(o_hop, zo_in.at[1], o_send.at[1, 4], o_recv.at[1, 4], z_peer(5))
            )

    near(0, 0, 4)
    near(1, 0, 2)
    relay(0)
    near(1, 2, 4)
    attend(0, 4, 0, 1)
    relay(1)
    far(0)
    attend(1, 4, 0, 1)
    across(0)
    far(1)
    across(1)
    o_down.wait_recv()
    z_copies[3].start()
    a_copies = []
    for h in range(2):
        mixed, top, total = joined(h, 0)
        for copy in z_copies[2 * h : 2 * h + 2]:
            copy.wait_recv()
        mixed, _, _ = mix(
            [mixed, zo_in[h]], [jnp.concatenate([top, total] * 4, axis=0), zs_in[h]]
        )
        att[h] = mixed.astype(jnp.bfloat16)
        a_copies.append(remote(att.at[h], att_in.at[h], a_send.at[h], a_recv.at[h], pair))
        a_copies[h].start()

    own = jnp.concatenate([att[0], att[1]], axis=1)
    for copy in w_copies + a_copies:
        copy.wait_recv()
    partner = jnp.concatenate([att_in[0], att_in[1]], axis=1)

    def share(d):
        start = pl.multiple_of((flip(zl, d) * 2 + c) * COLS, COLS)
        return jnp.dot(
            own, wo[:, pl.ds(start, COLS)], preferred_element_type=jnp.float32
        ) + jnp.dot(partner, wo_in[d], preferred_element_type=jnp.float32)

    r_copies = {}
    for d in (3, 2, 1):
        rs_out[d] = share(d).astype(jnp.bfloat16)
        r_copies[d] = remote(rs_out.at[d], rs_in.at[d], r_send.at[d], r_recv.at[d], tp_peer(d))
        r_copies[d].start()
    summed = hid[...].astype(jnp.float32) + share(0)
    for d in (1, 2, 3):
        r_copies[d].wait_recv()
        summed += rs_in[d].astype(jnp.float32)
    out_ref[...] = summed.astype(jnp.bfloat16)

    for copies in (h_copies, q_copies, r_copies):
        for copy in copies.values():
            copy.wait_send()
    for copy in sum(p_steps, []) + g_copies + z_copies + w_copies + a_copies + [q_down, o_down]:
        copy.wait_send()
    for h in range(2):
        for slot in (1, 2, 3, 5, 6, 7):
            for copy in returned(h, slot, slot % 4):
                copy.wait_send()


def local(
    hidden_in, w_query, w_keyval, w_out, prompt_cache, tail_cache, tail_table, tail_len, shared_len
):
    half = HD // 2
    freqs = 10000.0 ** (-np.arange(half, dtype=np.float64) / half)
    table = np.zeros((8, HD), np.float32)
    table[0] = np.concatenate([freqs, freqs])
    table[1] = np.concatenate([-np.ones(half), np.ones(half)])
    vmem = pl.BlockSpec(memory_space=pltpu.VMEM)
    smem = pl.BlockSpec(memory_space=pltpu.SMEM)
    anywhere = pl.BlockSpec(memory_space=pl.ANY)
    bf16, f32 = jnp.bfloat16, jnp.float32
    dma = pltpu.SemaphoreType.DMA
    block = (ROWS, COLS)
    out, cache = pl.pallas_call(
        kernel,
        out_shape=(
            jax.ShapeDtypeStruct(block, bf16),
            jax.ShapeDtypeStruct((ROWS, 2 * COLS), bf16),
        ),
        in_specs=[smem, smem, smem, vmem, anywhere, anywhere, anywhere, vmem, anywhere, vmem],
        out_specs=(vmem, vmem),
        scratch_shapes=[
            pltpu.VMEM((TPN,) + block, bf16),
            pltpu.VMEM((TPN * COLS, COLS), bf16),
            pltpu.VMEM((TPN * COLS, 2, COLS), bf16),
            pltpu.VMEM((TPN * COLS, 2 * COLS), bf16),
            pltpu.VMEM((COLS, TPN * COLS), bf16),
            pltpu.VMEM((ROWS, 2, COLS), bf16),
            pltpu.VMEM((KEYS, 2 * COLS), bf16),
            pltpu.VMEM((8, KEYS - ROWS), f32),
            pltpu.VMEM((2, 8, ROWS, HD), bf16),
            pltpu.VMEM((2, 8, ROWS, HD), bf16),
            pltpu.VMEM((2, 8, 8, ROWS), f32),
            pltpu.VMEM((2, 8, ROWS, HD), bf16),
            pltpu.VMEM((2, 8, 8, ROWS), f32),
            pltpu.VMEM((2, ROWS, HD), bf16),
            pltpu.VMEM((2, 8, ROWS), f32),
            pltpu.VMEM((2, ROWS, HD), bf16),
            pltpu.VMEM((2, 8, ROWS), f32),
            pltpu.VMEM((TPN,) + block, bf16),
            pltpu.VMEM((ROWS, HD), bf16),
            pltpu.VMEM((ROWS, HD), bf16),
            dma((2,)), dma((2,)),
            pltpu.VMEM((4,) + block, bf16),
            pltpu.VMEM((2, ROWS, HD), bf16),
            pltpu.VMEM((2, ROWS, HD), bf16),
            pltpu.VMEM((4,) + block, bf16),
            pltpu.VMEM((4,) + block, bf16),
            dma((4,)),
            dma((8,)), dma((8,)),
            dma((4,)), dma((4,)),
            dma((4,)), dma((4,)),
            dma((2, 8)), dma((2, 8)),
            dma((2, 8)), dma((2, 8)),
            dma((2, 8)), dma((2, 8)),
            dma((4,)), dma((4,)),
            dma((2,)), dma((2,)),
            dma((4,)), dma((4,)),
        ],
        compiler_params=pltpu.CompilerParams(collective_id=0, has_side_effects=True),
    )(
        shared_len,
        tail_len,
        tail_table,
        hidden_in,
        w_query,
        w_keyval,
        w_out,
        prompt_cache,
        tail_cache.reshape(ROWS, 2, COLS),
        jnp.asarray(table),
    )
    return (out, cache.reshape(ROWS, 2, COLS))


def solution(mesh):
    return jax.shard_map(
        local,
        mesh=mesh,
        in_specs=(
            P("seq", "tp"),
            P(None, "tp"),
            P(None, None, "tp"),
            P("tp", None),
            P("seq", None, "tp"),
            P("seq", None, None, "tp"),
            P(),
            P(),
            P(),
        ),
        out_specs=(P("seq", "tp"), P("seq", None, "tp")),
        check_vma=False,
    )
```

```python
import functools

import jax
import jax.numpy as jnp
import numpy as np
from jax import lax
from jax.experimental import pallas as pl
from jax.experimental.pallas import tpu as pltpu
from jax.sharding import PartitionSpec as P

HD = 128
REQ = 8
ROWS = 256
COLS = 256
TPN = 8
KEYS = 1536
NEG = -1e30
SCALE = HD**-0.5 * 1.4426950408889634
MESH = pl.DeviceIdType.MESH


def flip(v, d):
    low = (v % 2 + d % 2) % 2
    high = (v // 2 + d // 2) % 2
    return low + 2 * high


def slot_offsets(i):
    e = i // 4
    r = (i - 3 * e) % 4
    d = r + r // 2 - 2 * (r // 3)
    return d, e


def mix(parts, stats):
    top = functools.reduce(jnp.maximum, [s[0:2] for s in stats])
    raw = [s[2:4] * jnp.exp2(s[0:2] - top) for s in stats]
    total = sum(raw)
    weights = [w / total for w in raw]
    pad = jnp.zeros((128 - 2 * len(stats), ROWS), jnp.float32)
    columns = jnp.concatenate(weights + [pad], axis=0).T
    heads = []
    for h in range(2):
        lanes = slice(h * HD, (h + 1) * HD)
        heads.append(
            sum(
                columns[:, 2 * j + h : 2 * j + h + 1] * part[:, lanes].astype(jnp.float32)
                for j, part in enumerate(parts)
            )
        )
    return jnp.concatenate(heads, axis=1), top, total


def kernel(
    shared_ref, tail_len_ref, table_ref, hid, wq_hbm, wkv_hbm, wo_hbm, prompt, tail_hbm,
    freq_ref, out_ref, nc_ref,
    hbuf, wq, wkv_raw, wkv, wo, tail_raw, kv, bias, qbuf, obuf, sbuf, obuf_in, sbuf_in, zo, zs, zo_in, zs_in,
    wo_in, att, att_in, rs_out, rs_in,
    lsem, p_send, p_recv, h_send, h_recv, g_send, g_recv, q_send, q_recv, o_send, o_recv,
    s_send, s_recv, w_send, w_recv, a_send, a_recv, r_send, r_recv,
):
    s = lax.axis_index("seq")
    t = lax.axis_index("tp")
    y, x, zh = s // 8, (s // 2) % 4, s % 2
    zl, c = t // 2, t % 2
    member = s % 8
    pair = (s, zl * 2 + 1 - c)
    zpeer = (y * 8 + x * 2 + 1 - zh, t)

    def tp_peer(d):
        return (s, flip(zl, d) * 2 + c)

    def x_peer(d):
        return (y * 8 + flip(x, d) * 2 + zh, t)

    def y_peer(d):
        return (((y + d) % 8) * 8 + x * 2 + zh, t)

    def remote(src, dst, send, recv, device):
        return pltpu.make_async_remote_copy(
            src_ref=src, dst_ref=dst, send_sem=send, recv_sem=recv, device_id=device,
            device_id_type=MESH,
        )

    local = [
        pltpu.make_async_copy(wq_hbm, wq, lsem.at[0]),
        pltpu.make_async_copy(wkv_hbm, wkv_raw, lsem.at[1]),
        pltpu.make_async_copy(wo_hbm, wo, lsem.at[2]),
        pltpu.make_async_copy(tail_hbm, tail_raw, lsem.at[3]),
    ]
    for copy in local:
        copy.start()

    kv[pl.ds(512, 128), 0:COLS] = prompt[:, 0, :]
    kv[pl.ds(512, 128), COLS:] = prompt[:, 1, :]

    barrier = pltpu.get_barrier_semaphore()
    peers = [pair, zpeer]
    peers += [tp_peer(d) for d in (1, 2, 3)]
    peers += [x_peer(d) for d in (1, 2, 3)]
    peers += [y_peer(1), y_peer(7)]
    for peer in peers:
        pl.semaphore_signal(barrier, inc=1, device_id=peer, device_id_type=MESH)
    pl.semaphore_wait(barrier, len(peers))

    h_copies = {}
    for d in (3, 2, 1):
        h_copies[d] = remote(hid, hbuf.at[t], h_send.at[d], h_recv.at[d], tp_peer(d))
        h_copies[d].start()
    h_copies[0] = remote(hid, hbuf.at[t], h_send.at[0], h_recv.at[0], pair)
    h_copies[0].start()
    def ring(step):
        first = 64 if step == 4 else 128
        right = remote(
            kv.at[pl.ds(512 + (step - 1) * 128, first), :],
            kv.at[pl.ds(512 + step * 128, first), :],
            p_send.at[step - 1], p_recv.at[step - 1], y_peer(1),
        )
        shift = 128 - first
        left = remote(
            kv.at[pl.ds(512 + (9 - step) % 8 * 128 + shift, first), :],
            kv.at[pl.ds(512 + (8 - step) * 128 + shift, first), :],
            p_send.at[step + 3], p_recv.at[step + 3], y_peer(7),
        )
        return [right, left]

    p_steps = [ring(step) for step in (1, 2, 3, 4)]

    def forward(step):
        if step > 0:
            for copy in p_steps[step - 1]:
                copy.wait_recv()
        if step < 4:
            for copy in p_steps[step]:
                copy.start()

    forward(0)

    hbuf[t] = hid[...]
    own_tail = tail_len_ref[y]
    shared = shared_ref[0]
    lane = lax.broadcasted_iota(jnp.int32, (8, 128), 1)
    for k in range(2):
        block = jnp.int32(0)
        for j in range(16):
            block += jnp.where(table_ref[y, j] == s * 2 + k, jnp.int32(j), jnp.int32(0))
        bias[:, k * 128 : (k + 1) * 128] = jnp.where(block * 128 + lane < own_tail, 0.0, NEG)
    for d in range(8):
        start = (((y + 8 - d) % 8) * 8 + x * 2 + zh) * 128
        bias[:, 256 + d * 128 : 384 + d * 128] = jnp.where(start + lane < shared, 0.0, NEG)

    positions = shared + own_tail + member * ROWS
    positions = positions + lax.broadcasted_iota(jnp.int32, (ROWS, HD), 0)
    angles = positions.astype(jnp.float32) * freq_ref[0:1, :]
    cosine = jnp.cos(angles)
    sine = jnp.sin(angles) * freq_ref[1:2, :]
    local[3].wait()
    kv[pl.ds(256, 256), 0:COLS] = tail_raw[:, 0, :]
    kv[pl.ds(256, 256), COLS:] = tail_raw[:, 1, :]
    local[1].wait()

    def unweave(k, carry):
        rows = pl.ds(pl.multiple_of(k * 256, 256), 256)
        wkv[rows, 0:COLS] = wkv_raw[rows, 0, :]
        wkv[rows, COLS:] = wkv_raw[rows, 1, :]
        return carry

    lax.fori_loop(0, 4, unweave, 0)
    forward(1)
    lax.fori_loop(4, 8, unweave, 0)
    forward(2)

    g_copies = []
    for d in (1, 2, 3):
        h_copies[d].wait_recv()
        index = flip(zl, d) * 2 + c
        copy = remote(hbuf.at[index], hbuf.at[index], g_send.at[d], g_recv.at[d], pair)
        copy.start()
        g_copies.append(copy)
    forward(3)
    h_copies[0].wait_recv()
    for copy in g_copies:
        copy.wait_recv()

    total = functools.reduce(
        jnp.add, [hbuf[j].astype(jnp.float32) for j in range(TPN)]
    )
    mean = jnp.sum(total, axis=1, keepdims=True) * (1.0 / (TPN * COLS))
    square = jnp.zeros((ROWS, COLS), jnp.float32)
    for j in range(TPN):
        centred = hbuf[j].astype(jnp.float32) - mean
        square += centred * centred
    spread = jnp.sum(square, axis=1, keepdims=True) * (1.0 / (TPN * COLS))
    factor = lax.rsqrt(spread + 1e-05)
    local[0].wait()
    query = jnp.zeros((ROWS, COLS), jnp.float32)
    keyval = jnp.zeros((ROWS, 2 * COLS), jnp.float32)
    for j in range(TPN):
        normed = ((hbuf[j].astype(jnp.float32) - mean) * factor).astype(jnp.bfloat16)
        rows = pl.ds(j * COLS, COLS)
        query += jnp.dot(normed, wq[rows, :], preferred_element_type=jnp.float32)
        keyval += jnp.dot(normed, wkv[rows, :], preferred_element_type=jnp.float32)

    def rotated(vectors):
        return (vectors * cosine + pltpu.roll(vectors, HD // 2, 1) * sine).astype(jnp.bfloat16)

    for h in range(2):
        lanes = slice(h * HD, (h + 1) * HD)
        qbuf[0, :, lanes] = rotated(query[:, lanes])
    q_copies = {7: remote(qbuf.at[0], qbuf.at[7], q_send.at[7], q_recv.at[7], zpeer)}
    q_copies[7].start()
    for i in (1, 2, 3):
        d, _ = slot_offsets(i)
        q_copies[i] = remote(qbuf.at[0], qbuf.at[i], q_send.at[i], q_recv.at[i], x_peer(d))
        q_copies[i].start()
    for i in (4, 5, 6):
        d, _ = slot_offsets(i)
        q_copies[i] = remote(qbuf.at[7], qbuf.at[i], q_send.at[i], q_recv.at[i], x_peer(d))
    local[2].wait()
    w_copies = []
    for d in range(4):
        start = pl.multiple_of((flip(zl, d) * 2 + 1 - c) * COLS, COLS)
        w_copies.append(
            remote(wo.at[:, pl.ds(start, COLS)], wo_in.at[d], w_send.at[d], w_recv.at[d], pair)
        )
        w_copies[d].start()
    for h in range(2):
        lanes = slice(h * HD, (h + 1) * HD)
        new_key = rotated(keyval[:, lanes])
        kv[pl.ds(0, ROWS), lanes] = new_key
        nc_ref[:, lanes] = new_key
    new_value = keyval[:, COLS:].astype(jnp.bfloat16)
    kv[pl.ds(0, ROWS), COLS:] = new_value
    nc_ref[:, COLS:] = new_value
    forward(4)

    def block(i, carry):
        d, e = slot_offsets(i)
        other = flip(x, d) * 2 + (zh + e) % 2

        @pl.when(i == 2)
        def _():
            q_copies[7].wait_recv()
            for k in (4, 5, 6):
                q_copies[k].start()

        @pl.when((i > 0) & (i < 7))
        def _():
            remote(qbuf.at[0], qbuf.at[i], q_send.at[i], q_recv.at[i], x_peer(d)).wait_recv()

        column = lax.broadcasted_iota(jnp.int32, (ROWS, ROWS), 1)
        row = lax.broadcasted_iota(jnp.int32, (ROWS, ROWS), 0)
        causal = column - row <= (other - member) * ROWS
        tops, totals = [], []
        for h in range(2):
            lanes = slice(h * HD, (h + 1) * HD)
            q = qbuf[i, :, lanes]
            scores = lax.dot_general(
                q, kv[:, lanes], (((1,), (1,)), ((), ())), preferred_element_type=jnp.float32
            ) * SCALE
            fresh = jnp.where(causal, scores[:, :ROWS], NEG)
            cached = scores[:, ROWS:] + bias[0:1, :]
            top = jnp.maximum(
                jnp.max(fresh, axis=1, keepdims=True), jnp.max(cached, axis=1, keepdims=True)
            )
            fresh = jnp.exp2(fresh - top)
            cached = jnp.exp2(cached - top)
            total = jnp.sum(fresh, axis=1, keepdims=True) + jnp.sum(cached, axis=1, keepdims=True)
            mixed = jnp.dot(
                fresh.astype(jnp.bfloat16), kv[0:ROWS, COLS + h * HD : COLS + (h + 1) * HD],
                preferred_element_type=jnp.float32,
            ) + jnp.dot(
                cached.astype(jnp.bfloat16), kv[ROWS:KEYS, COLS + h * HD : COLS + (h + 1) * HD],
                preferred_element_type=jnp.float32,
            )
            obuf[i, :, lanes] = (mixed / total).astype(jnp.bfloat16)
            tops.append(top)
            totals.append(total)
        place = lax.broadcasted_iota(jnp.int32, (ROWS, 128), 1)
        packed = jnp.where(
            place == 0,
            tops[0],
            jnp.where(place == 1, tops[1], jnp.where(place == 2, totals[0], totals[1])),
        )
        sbuf[i] = packed.T[0:8]

        @pl.when((i > 0) & (i < 7))
        def _():
            remote(sbuf.at[i], sbuf_in.at[i], s_send.at[i], s_recv.at[i], x_peer(d)).start()
            remote(obuf.at[i], obuf_in.at[i], o_send.at[i], o_recv.at[i], x_peer(d)).start()

        return carry

    lax.fori_loop(0, 8, block, 0)

    def returned(i):
        d, _ = slot_offsets(i)
        return (
            remote(sbuf.at[i], sbuf_in.at[i], s_send.at[i], s_recv.at[i], x_peer(d)),
            remote(obuf.at[i], obuf_in.at[i], o_send.at[i], o_recv.at[i], x_peer(d)),
        )

    def joined(own, others):
        for i in others:
            for copy in returned(i):
                copy.wait_recv()
        return mix(
            [obuf[own]] + [obuf_in[i] for i in others], [sbuf[own]] + [sbuf_in[i] for i in others]
        )

    mixed, top, total = joined(7, (4, 5, 6))
    zo[...] = mixed.astype(jnp.bfloat16)
    zs[...] = jnp.concatenate([top, total, top, total], axis=0)
    z_copies = [
        remote(zs, zs_in, s_send.at[7], s_recv.at[7], zpeer),
        remote(zo, zo_in, o_send.at[7], o_recv.at[7], zpeer),
    ]
    for copy in z_copies:
        copy.start()
    mixed, top, total = joined(0, (1, 2, 3))
    for copy in z_copies:
        copy.wait_recv()
    mixed, _, _ = mix(
        [mixed, zo_in[...]], [jnp.concatenate([top, total], axis=0), zs_in[...]]
    )
    att[...] = mixed.astype(jnp.bfloat16)
    a_copy = remote(att, att_in, a_send.at[0], a_recv.at[0], pair)
    a_copy.start()

    for copy in w_copies + [a_copy]:
        copy.wait_recv()

    def share(d):
        start = pl.multiple_of((flip(zl, d) * 2 + c) * COLS, COLS)
        return jnp.dot(
            att[...], wo[:, pl.ds(start, COLS)], preferred_element_type=jnp.float32
        ) + jnp.dot(att_in[...], wo_in[d], preferred_element_type=jnp.float32)

    r_copies = {}
    for d in (3, 2, 1):
        rs_out[d] = share(d).astype(jnp.bfloat16)
        r_copies[d] = remote(rs_out.at[d], rs_in.at[d], r_send.at[d], r_recv.at[d], tp_peer(d))
        r_copies[d].start()
    summed = hid[...].astype(jnp.float32) + share(0)
    for d in (1, 2, 3):
        r_copies[d].wait_recv()
        summed += rs_in[d].astype(jnp.float32)
    out_ref[...] = summed.astype(jnp.bfloat16)

    for copies in (h_copies, q_copies, r_copies):
        for copy in copies.values():
            copy.wait_send()
    for copy in sum(p_steps, []) + g_copies + z_copies + w_copies + [a_copy]:
        copy.wait_send()
    for i in range(1, 7):
        for copy in returned(i):
            copy.wait_send()


def local(
    hidden_in, w_query, w_keyval, w_out, prompt_cache, tail_cache, tail_table, tail_len, shared_len
):
    half = HD // 2
    freqs = 10000.0 ** (-np.arange(half, dtype=np.float64) / half)
    table = np.zeros((8, HD), np.float32)
    table[0] = np.concatenate([freqs, freqs])
    table[1] = np.concatenate([-np.ones(half), np.ones(half)])
    vmem = pl.BlockSpec(memory_space=pltpu.VMEM)
    smem = pl.BlockSpec(memory_space=pltpu.SMEM)
    anywhere = pl.BlockSpec(memory_space=pl.ANY)
    bf16, f32 = jnp.bfloat16, jnp.float32
    dma = pltpu.SemaphoreType.DMA
    block = (ROWS, COLS)
    out, cache = pl.pallas_call(
        kernel,
        out_shape=(
            jax.ShapeDtypeStruct(block, bf16),
            jax.ShapeDtypeStruct((ROWS, 2 * COLS), bf16),
        ),
        in_specs=[smem, smem, smem, vmem, anywhere, anywhere, anywhere, vmem, anywhere, vmem],
        out_specs=(vmem, vmem),
        scratch_shapes=[
            pltpu.VMEM((TPN,) + block, bf16),
            pltpu.VMEM((TPN * COLS, COLS), bf16),
            pltpu.VMEM((TPN * COLS, 2, COLS), bf16),
            pltpu.VMEM((TPN * COLS, 2 * COLS), bf16),
            pltpu.VMEM((COLS, TPN * COLS), bf16),
            pltpu.VMEM((ROWS, 2, COLS), bf16),
            pltpu.VMEM((KEYS, 2 * COLS), bf16),
            pltpu.VMEM((8, KEYS - ROWS), f32),
            pltpu.VMEM((8,) + block, bf16),
            pltpu.VMEM((8,) + block, bf16),
            pltpu.VMEM((8, 8, ROWS), f32),
            pltpu.VMEM((8,) + block, bf16),
            pltpu.VMEM((8, 8, ROWS), f32),
            pltpu.VMEM(block, bf16),
            pltpu.VMEM((8, ROWS), f32),
            pltpu.VMEM(block, bf16),
            pltpu.VMEM((8, ROWS), f32),
            pltpu.VMEM((4,) + block, bf16),
            pltpu.VMEM(block, bf16),
            pltpu.VMEM(block, bf16),
            pltpu.VMEM((4,) + block, bf16),
            pltpu.VMEM((4,) + block, bf16),
            dma((4,)),
            dma((8,)), dma((8,)),
            dma((4,)), dma((4,)),
            dma((4,)), dma((4,)),
            dma((8,)), dma((8,)),
            dma((8,)), dma((8,)),
            dma((8,)), dma((8,)),
            dma((4,)), dma((4,)),
            dma((1,)), dma((1,)),
            dma((4,)), dma((4,)),
        ],
        compiler_params=pltpu.CompilerParams(collective_id=0, has_side_effects=True),
    )(
        shared_len,
        tail_len,
        tail_table,
        hidden_in,
        w_query,
        w_keyval,
        w_out,
        prompt_cache,
        tail_cache.reshape(ROWS, 2, COLS),
        jnp.asarray(table),
    )
    return (out, cache.reshape(ROWS, 2, COLS))


def solution(mesh):
    return jax.shard_map(
        local,
        mesh=mesh,
        in_specs=(
            P("seq", "tp"),
            P(None, "tp"),
            P(None, None, "tp"),
            P("tp", None),
            P("seq", None, "tp"),
            P("seq", None, None, "tp"),
            P(),
            P(),
            P(),
        ),
        out_specs=(P("seq", "tp"), P("seq", None, "tp")),
        check_vma=False,
    )
```
